32 devices in a mesh: groups: 2 (over y), slices: 8 (over z, x), ering: 2 (over core).
Axes of the slice: x: 2, y: 2, z: 4, core: 2. Of those that a mesh axis runs over, the one named last changes fastest.
Arguments:
- positions: float32 [3, 128, 256], P(None, ('groups', 'slices'), 'ering'), parts along dimension 1, may hold values from -9 to 9
- hidden: bfloat16 [128, 256, 256], P(('groups', 'slices'), 'ering'), parts along dimension 0, may hold values from -6 to 6
- cotangent: bfloat16 [128, 256, 256], P(('groups', 'slices'), 'ering'), parts along dimension 0, may hold values from -6 to 6
- embed_weight: float32 [32, 4], replicated, may hold values from -3 to 3
- embed_bias: float32 [32], replicated, may hold values from -3 to 3
- pair_weight: bfloat16 [32, 32], replicated, may hold values from -1 to 1
- pair_bias: float32 [32], replicated, may hold values from -3 to 3
- one_weight: bfloat16 [256, 256], replicated, may hold values from -0.375 to 0.375
- pool_weight: bfloat16 [32, 256], replicated, may hold values from -1 to 1
- mean_weight: bfloat16 [256, 256], replicated, may hold values from -0.375 to 0.375
- one_bias: float32 [256], replicated, may hold values from -3 to 3
- drift_weight: bfloat16 [3, 256], replicated, may hold values from -0.375 to 0.375
Outputs:
- updated: bfloat16 [128, 256, 256], P(('groups', 'slices'), 'ering'), parts along dimension 0
- hidden_grad: bfloat16 [128, 256, 256], P(('groups', 'slices'), 'ering'), parts along dimension 0
- link_terms: float32 [128, 256], P(('groups', 'slices'), 'ering'), parts along dimension 0
- pair_grad: float32 [64, 32], P('groups'), parts along dimension 0
- bias_grad: float32 [64], P('groups'), parts along dimension 0
- one_grad: float32 [512, 256], P('groups'), parts along dimension 0
- pool_grad: float32 [64, 256], P('groups'), parts along dimension 0
- mean_grad: float32 [512, 256], P('groups'), parts along dimension 0
The draws below stay inside these ranges and needn't reach their ends.
There are 2 independent parts, one for each index of `groups`. The reference program is written for one: setup_inputs(seed, part) draws one part's arguments, and reference() takes and returns one part's arrays. A program takes and returns all parts, laid end to end along the dimension named above; an argument that names none is the same for every part. Nothing has to cross between parts.
All inputs are finite; a program needn't handle non-finite values.
Results may differ from the reference program's by a relative error of at most 0.0054.
Values may be sent and summed in bfloat16 or wider, within the bound.
No kernel may reach another device: no remote copies, remote signals or barrier semaphores. Data moves between devices by JAX's collectives and lax.ppermute only.
A program may use at most 64 MiB of HBM per device.

```python
import math
import jax
import jax.numpy as jnp
from jax import lax

NE = 256
D1 = 256
PW = 32
SLICES = 64


def steps_of(stream_key, extent, split, least, high):
    factor_of = 1.0
    for axis_at, parts in split:
        draws = jax.random.uniform(jax.random.fold_in(jax.random.fold_in(stream_key, 6), axis_at), (parts,), jnp.float32, least / len(split), high / len(split))
        factor_of = factor_of * jnp.repeat(jnp.exp(draws), extent[axis_at] // parts).reshape((-1,) + (1,) * (len(extent) - 1 - axis_at))
    return factor_of


def bell_draw(stream_key, extent, spread, reach, cuts=(), dtype=jnp.bfloat16):
    entries = jax.random.normal(stream_key, extent, jnp.float32) * spread
    if len(cuts) > 0:
        entries = steps_of(stream_key, extent, cuts, -0.22, 0.18) * entries
    return jnp.clip(entries, min=-reach, max=reach).astype(dtype)


def setup_inputs(seed: int = 0, part: int = 0) -> dict:
    key_of = jax.random.split(jax.random.key(seed), 13)
    part_splits = jax.random.split(jax.random.fold_in(key_of[12], part), 13)
    positions = bell_draw(part_splits[0], (3, SLICES, NE), 1.5, 9.0, ((1, 8), (2, 2)), jnp.float32)
    hidden = bell_draw(part_splits[1], (SLICES, NE, D1), 1.0, 6.0, ((0, 8), (1, 2)))
    cotangent = bell_draw(part_splits[2], (SLICES, NE, D1), 1.0, 6.0, ((0, 8), (1, 2)))
    embed_weight = bell_draw(key_of[3], (PW, 4), 4 ** -0.5, 3.0, (), jnp.float32)
    embed_bias = bell_draw(key_of[4], (PW,), 0.5, 3.0, (), jnp.float32)
    pair_weight = bell_draw(key_of[5], (PW, PW), PW ** -0.5, 1.0)
    pair_bias = bell_draw(key_of[6], (PW,), 0.5, 3.0, (), jnp.float32)
    one_weight = bell_draw(key_of[7], (D1, D1), D1 ** -0.5, 0.375)
    pool_weight = bell_draw(key_of[8], (PW, D1), PW ** -0.5, 1.0)
    mean_weight = bell_draw(key_of[9], (D1, D1), D1 ** -0.5, 0.375)
    one_bias = bell_draw(key_of[10], (D1,), 0.5, 3.0, (), jnp.float32)
    drift_weight = bell_draw(key_of[11], (3, D1), D1 ** -0.5, 0.375)
    return dict(positions=positions, hidden=hidden, cotangent=cotangent, embed_weight=embed_weight, embed_bias=embed_bias, pair_weight=pair_weight, pair_bias=pair_bias, one_weight=one_weight, pool_weight=pool_weight, mean_weight=mean_weight, one_bias=one_bias, drift_weight=drift_weight)


HIGH = lax.Precision.HIGHEST
step_tau = 0.5

def pair_block(own_pos, all_pos, embed_weight, embed_bias, pair_weight, pair_bias):
    offsets = own_pos[:, :, None] - all_pos[:, None, :]
    radial = jnp.sqrt(lax.optimization_barrier(jnp.sum(offsets * offsets, axis=0)) + 1.0)
    features = jnp.concatenate([offsets, radial[None]], axis=0)
    pair_in = jnp.tanh(jnp.einsum('ck,kij->cij', embed_weight, features, precision=HIGH) + embed_bias[:, None, None]).astype(jnp.bfloat16)
    pair_pre = jnp.einsum('ck,kij->cij', pair_weight.astype(jnp.float32), pair_in.astype(jnp.float32), precision=HIGH) + pair_bias[:, None, None]
    pair_act = jnp.tanh(pair_pre)
    pooled = lax.optimization_barrier(jnp.mean(pair_act + pair_in.astype(jnp.float32), axis=2)).T.astype(jnp.bfloat16)
    return (pair_in, pair_act, pooled)

def reference(positions, hidden, cotangent, embed_weight, embed_bias, pair_weight, pair_bias, one_weight, pool_weight, mean_weight, one_bias, drift_weight):

    def one_slice(carry, inputs):
        pos_s, hid_s, cot_s = inputs
        pair_in, pair_act, pooled = pair_block(pos_s, pos_s, embed_weight, embed_bias, pair_weight, pair_bias)
        mean_rows = (lax.optimization_barrier(jnp.sum(hid_s.astype(jnp.float32), axis=0)) / NE).astype(jnp.bfloat16)
        one_pre = jnp.dot(hid_s, one_weight, preferred_element_type=jnp.float32)
        one_pre = one_pre + jnp.dot(pooled, pool_weight, preferred_element_type=jnp.float32)
        one_pre = one_pre + jnp.dot(mean_rows[None, :], mean_weight, preferred_element_type=jnp.float32) + one_bias
        one_act = jnp.tanh(one_pre)
        updated = (one_act + hid_s.astype(jnp.float32)).astype(jnp.bfloat16)
        pre_grad = (cot_s.astype(jnp.float32) * (1.0 - one_act * one_act)).astype(jnp.bfloat16)
        column_sum = lax.optimization_barrier(jnp.sum(pre_grad.astype(jnp.float32), axis=0))
        pooled_grad = jnp.dot(pre_grad, pool_weight.T, preferred_element_type=jnp.float32)
        mean_back = jnp.dot(column_sum[None, :], mean_weight.astype(jnp.float32).T, precision=HIGH)
        hidden_grad = (cot_s.astype(jnp.float32) + jnp.dot(pre_grad, one_weight.T, preferred_element_type=jnp.float32) + mean_back / NE).astype(jnp.bfloat16)
        act_grad = pooled_grad.T[:, :, None] / NE * (1.0 - pair_act * pair_act)
        act_low = act_grad.astype(jnp.bfloat16)
        weight_term = jnp.einsum('cij,kij->ck', act_low.astype(jnp.float32), pair_in.astype(jnp.float32), precision=HIGH)
        bias_term = lax.optimization_barrier(jnp.sum(act_grad, axis=(1, 2)))
        carry = (carry[0] + weight_term, carry[1] + bias_term, carry[2] + jnp.dot(hid_s.T, pre_grad, preferred_element_type=jnp.float32), carry[3] + jnp.dot(pooled.T, pre_grad, preferred_element_type=jnp.float32), carry[4] + mean_rows.astype(jnp.float32)[:, None] * column_sum[None, :])
        return (carry, (updated, hidden_grad))
    start = (jnp.zeros((PW, PW), jnp.float32), jnp.zeros((PW,), jnp.float32), jnp.zeros((D1, D1), jnp.float32), jnp.zeros((PW, D1), jnp.float32), jnp.zeros((D1, D1), jnp.float32))
    totals, (updated, hidden_grad) = lax.scan(one_slice, start, (jnp.moveaxis(positions, 1, 0), hidden, cotangent))
    scale = 1.0 / math.sqrt(SLICES * NE)
    drift = jnp.einsum('cd,sid->csi', drift_weight.astype(jnp.float32), updated.astype(jnp.float32), precision=HIGH)
    following = jnp.concatenate([positions[:, 1:], jnp.zeros((3, 1, NE), jnp.float32)], axis=1)
    jump = following - positions - step_tau * drift
    link_terms = lax.optimization_barrier(jnp.sum(jump * jump, axis=0)) / (12.0 * step_tau)
    last_row = jnp.arange(SLICES) == SLICES - 1
    link_terms = jnp.where(last_row[:, None], jnp.float32(0.0), link_terms)
    return (updated, hidden_grad, link_terms, scale * totals[0], scale * totals[1], scale * totals[2], scale * totals[3], scale * totals[4])
```

```python
import math

import jax
import jax.numpy as jnp
from jax import lax
from jax.experimental import pallas as pl
from jax.experimental.pallas import tpu as pltpu
from jax.sharding import PartitionSpec as P

HIGH = lax.Precision.HIGHEST
f32 = jnp.float32
bf16 = jnp.bfloat16
step_tau = 0.5
VMEM_LIMIT = 56 << 20


def dot(a, b, ca, cb, precision=None):
    return lax.dot_general(
        a, b, (((ca,), (cb,)), ((), ())), preferred_element_type=f32, precision=precision
    )


def split3(x):
    first = x.astype(bf16).astype(f32)
    rest = x - first
    second = rest.astype(bf16).astype(f32)
    return first, second, rest - second


def iota(shape, dim):
    return lax.broadcasted_iota(jnp.int32, shape, dim)


def pair_kernel(
    own_ref, other_ref, ew_ref, eb_ref, pw_ref, pb_ref,
    pooled_ref, h_ref, g_ref,
    embed_mat, block_mat, a_rows, feat, bias_row,
):
    s = pl.program_id(0)

    @pl.when(s == 0)
    def _():
        wide = jnp.concatenate([ew_ref[...].T] * 8, axis=1)
        w1, w2, w3 = split3(wide)
        row = iota((256, 256), 0)
        lane = iota((256, 256), 1)
        for g in range(8):
            hit = (row % 64 == g * 8 + lane // 32) & (row < 192)
            out = jnp.where(hit, jnp.where(row < 128, w1[3:4, :], w2[3:4, :]), 0.0)
            pieces = (w1, w2, w3, w1, w2, w1)
            for c in range(3):
                for p in range(6):
                    out = jnp.where(row == 192 + 6 * c + p, -pieces[p][c : c + 1, :], out)
            embed_mat[:, g * 256 : (g + 1) * 256] = out.astype(bf16)
        tiled = jnp.concatenate([pw_ref[...].astype(f32).T] * 8, axis=1)
        tiled = jnp.concatenate([tiled] * 8, axis=0)
        block_mat[...] = jnp.where(row // 32 == lane // 32, tiled, 0.0).astype(bf16)
        bias_row[...] = jnp.broadcast_to(jnp.concatenate([pb_ref[...]] * 8, axis=1), (8, 256))
        wide_bias = jnp.concatenate([eb_ref[...]] * 8, axis=1)
        electron = iota((128, 256), 0)
        lane128 = iota((128, 256), 1)
        for g in range(16):
            pick = jnp.where(electron == g * 8 + lane128 // 32, 1.0, 0.0).astype(bf16)
            total = jnp.broadcast_to(wide_bias, (own_ref.shape[1], 256))
            for c in range(3):
                spread = sum(dot(q.astype(bf16), pick, 1, 0) for q in split3(own_ref[c]))
                total = total + spread * wide[c : c + 1, :]
            a_rows[:, g * 256 : (g + 1) * 256] = total

    lane = iota((256, 128), 1)
    square = jnp.ones((256, 128), f32)
    misc = jnp.zeros((256, 128), f32)
    rows = [own_ref[c, pl.ds(s, 1), :] for c in range(3)]
    others = [other_ref[c, pl.ds(s, 1), :] for c in range(3)]
    stacked = jnp.concatenate(
        [jnp.concatenate([rows[c], others[c]], axis=1) for c in range(3)]
        + [jnp.zeros((5, 256), f32)],
        axis=0,
    )
    columns = stacked.T
    for c in range(3):
        spread = jnp.broadcast_to(columns[:, c : c + 1], (256, 128))
        offset = spread - rows[c]
        square = square + offset * offset
        s1, s2, s3 = split3(spread)
        base = 64 + 6 * c
        misc = jnp.where((lane >= base) & (lane < base + 3), s1, misc)
        misc = jnp.where((lane >= base + 3) & (lane < base + 5), s2, misc)
        misc = jnp.where(lane == base + 5, s3, misc)
    radial = jnp.sqrt(square)
    high = radial.astype(bf16).astype(f32)
    low = radial - high
    high_turned = pltpu.roll(high, 64, 1)
    low_turned = pltpu.roll(low, 64, 1)
    left = lane < 64
    feat[0, :, :128] = jnp.where(left, high, low_turned).astype(bf16)
    feat[0, :, 128:] = jnp.where(left, high, misc).astype(bf16)
    feat[1, :, :128] = jnp.where(left, high_turned, low).astype(bf16)
    feat[1, :, 128:] = jnp.where(left, high_turned, misc).astype(bf16)
    diagonal = iota((8, 256), 0) == iota((8, 256), 1) // 32
    block = iota((32, 256), 1) // 32
    for g in range(16):
        half, inner = g // 8, g % 8
        pre = dot(feat[half], embed_mat[:, inner * 256 : (inner + 1) * 256], 1, 0)
        pre = pre + a_rows[pl.ds(s, 1), g * 256 : (g + 1) * 256]
        wide_in = jnp.tanh(pre)
        pair_in = wide_in.astype(bf16)
        act = jnp.tanh(dot(pair_in, block_mat[...], 1, 0) + bias_row[0:1, :])
        mean = jnp.sum(wide_in + act, axis=0, keepdims=True) * (1.0 / 256)
        slope = 1.0 - act * act
        h_ref[0, g : g + 1, :] = jnp.sum(slope, axis=0, keepdims=True)
        pooled_ref[0, g * 8 : (g + 1) * 8, :] = jnp.where(diagonal, mean, 0.0)
        outer = dot(pair_in, slope.astype(bf16), 0, 0)
        picked = outer[0:32]
        for q in range(1, 8):
            picked = jnp.where(block == q, outer[q * 32 : (q + 1) * 32], picked)
        g_ref[0, g * 32 : (g + 1) * 32, :] = picked


def pair_call(own, other, ew, eb, pw, pb):
    count = own.shape[1]
    args = (own, other, ew, eb.reshape(1, 32), pw, pb.reshape(1, 32))
    return pl.pallas_call(
        pair_kernel,
        grid=(count,),
        in_specs=[pl.BlockSpec(a.shape, lambda s, n=a.ndim: (0,) * n) for a in args],
        out_specs=[
            pl.BlockSpec((1, 128, 256), lambda s: (s, 0, 0)),
            pl.BlockSpec((1, 16, 256), lambda s: (s, 0, 0)),
            pl.BlockSpec((1, 512, 256), lambda s: (s, 0, 0)),
        ],
        out_shape=[
            jax.ShapeDtypeStruct((count, 128, 256), f32),
            jax.ShapeDtypeStruct((count, 16, 256), f32),
            jax.ShapeDtypeStruct((count, 512, 256), f32),
        ],
        scratch_shapes=[
            pltpu.VMEM((256, 2048), bf16),
            pltpu.VMEM((256, 256), bf16),
            pltpu.VMEM((count, 4096), f32),
            pltpu.VMEM((2, 256, 256), bf16),
            pltpu.VMEM((8, 256), f32),
        ],
        compiler_params=pltpu.CompilerParams(vmem_limit_bytes=VMEM_LIMIT),
        name="pair_stage",
    )(*args)


RED = 336
HALF = RED // 2


def one_kernel(
    core_ref, hid_ref, cot_ref, pooled_ref, h_ref, g_ref, sum_a_ref, sum_b_ref,
    ow_ref, qw_ref, mw_ref, ob_ref,
    updated_ref, pre_ref, keep_ref, send_ref, mean_ref,
    red,
):
    count = sum_a_ref.shape[0]
    mean_rows = ((sum_a_ref[...] + sum_b_ref[...]) * (1.0 / 256)).astype(bf16)
    mean_ref[...] = mean_rows.astype(f32)
    per_slice = dot(mean_rows, mw_ref[...], 1, 0) + ob_ref[...]
    pool_tiled = jnp.concatenate([qw_ref[...]] * 8, axis=0)
    one_total = jnp.zeros((256, 256), f32)
    pool_total = jnp.zeros((256, 256), f32)
    pair_total = jnp.zeros((32, 256), f32)
    bias_total = jnp.zeros((16, 256), f32)
    own_lanes = iota((128, 256), 0) % 8 == iota((128, 256), 1) // 32
    parts = []
    for s in range(count):
        at = slice(s * 128, (s + 1) * 128)
        hid = hid_ref[at, :]
        pooled = pooled_ref[at, :].astype(bf16)
        pre = dot(hid, ow_ref[...], 1, 0) + dot(pooled, pool_tiled, 1, 0) + per_slice[s : s + 1, :]
        act = jnp.tanh(pre)
        updated_ref[at, :] = (act + hid.astype(f32)).astype(bf16)
        grad = (cot_ref[at, :].astype(f32) * (1.0 - act * act)).astype(bf16)
        pre_ref[at, :] = grad
        parts.append(jnp.sum(grad.astype(f32), axis=0, keepdims=True))
        one_total = one_total + dot(hid, grad, 0, 0)
        pool_total = pool_total + dot(pooled, grad, 0, 0)
        back = jnp.where(own_lanes, dot(grad, pool_tiled, 1, 1), 0.0)
        back = jnp.sum(back.reshape(16, 8, 256), axis=1)
        bias_total = bias_total + back * h_ref[s * 16 : (s + 1) * 16, :]
        for g in range(16):
            base = s * 512 + g * 32
            pair_total = pair_total + g_ref[base : base + 32, :] * back[g : g + 1, :]
    fold = jnp.where(iota((256, 128), 0) % 32 == iota((256, 128), 1), 1.0, 0.0)
    pool = pool_total[0:32]
    for q in range(1, 8):
        pool = pool + pool_total[q * 32 : (q + 1) * 32]
    bias_one = jnp.broadcast_to(jnp.sum(bias_total, axis=0, keepdims=True), (16, 256))
    red[0:256, :] = one_total
    red[256:288, :] = pool
    red[288:336, :] = jnp.zeros((48, 256), f32)
    red[288:320, 0:128] = dot(pair_total, fold, 1, 0, HIGH)
    red[320:336, 0:128] = dot(bias_one, fold, 1, 0, HIGH)
    core = core_ref[0]
    keep_ref[...] = red[pl.ds(pl.multiple_of(core * HALF, 8), HALF), :]
    send_ref[0:HALF, :] = red[pl.ds(pl.multiple_of((1 - core) * HALF, 8), HALF), :]
    send_ref[HALF:, :] = jnp.concatenate(parts, axis=0)
    mean_ref[...] = mean_rows.astype(f32)


def one_call(core, hid, cot, pooled, h_sums, g_sums, sum_a, sum_b, ow, qw, mw, ob):
    rows = hid.shape[0]
    count = sum_a.shape[0]
    args = (core, hid, cot, pooled, h_sums, g_sums, sum_a, sum_b, ow, qw, mw, ob.reshape(1, 256))
    whole = pl.BlockSpec(memory_space=pltpu.VMEM)
    return pl.pallas_call(
        one_kernel,
        in_specs=[pl.BlockSpec(memory_space=pltpu.SMEM)] + [whole] * (len(args) - 1),
        out_specs=[whole] * 5,
        out_shape=[
            jax.ShapeDtypeStruct((rows, 256), bf16),
            jax.ShapeDtypeStruct((rows, 256), bf16),
            jax.ShapeDtypeStruct((HALF, 256), f32),
            jax.ShapeDtypeStruct((HALF + count, 256), f32),
            jax.ShapeDtypeStruct((count, 256), f32),
        ],
        scratch_shapes=[pltpu.VMEM((RED, 256), f32)],
        compiler_params=pltpu.CompilerParams(vmem_limit_bytes=VMEM_LIMIT),
        name="one_stage",
    )(*args)


def back_kernel(
    cot_ref, pre_ref, upd_ref, col_ref, pos_ref, ow_ref, mw_ref, dw_ref,
    grad_ref, link_ref, last_ref,
):
    count = col_ref.shape[0]
    back = dot(col_ref[...], mw_ref[...].astype(f32), 1, 1, HIGH) * (1.0 / 256)
    drifts = []
    for s in range(count):
        at = slice(s * 128, (s + 1) * 128)
        grad = cot_ref[at, :].astype(f32) + dot(pre_ref[at, :], ow_ref[...], 1, 1)
        grad_ref[at, :] = (grad + back[s : s + 1, :]).astype(bf16)
        drifts.append(dot(dw_ref[...], upd_ref[at, :], 1, 1))
    for s in range(count):
        here = [-pos_ref[c, s : s + 1, :] - step_tau * drifts[s][c : c + 1, :] for c in range(3)]
        if s < count - 1:
            jumps = [here[c] + pos_ref[c, s + 1 : s + 2, :] for c in range(3)]
            total = jumps[0] * jumps[0] + jumps[1] * jumps[1] + jumps[2] * jumps[2]
            link_ref[s : s + 1, :] = total * (1.0 / (12.0 * step_tau))
        else:
            link_ref[s : s + 1, :] = jnp.zeros((1, 128), f32)
            last_ref[...] = jnp.concatenate(here + [jnp.zeros((5, 128), f32)], axis=0)


def back_call(cot, pre, updated, col, pos, ow, mw, dw):
    whole = pl.BlockSpec(memory_space=pltpu.VMEM)
    args = (cot, pre, updated, col, pos, ow, mw, dw)
    return pl.pallas_call(
        back_kernel,
        in_specs=[whole] * len(args),
        out_specs=[whole] * 3,
        out_shape=[
            jax.ShapeDtypeStruct(cot.shape, bf16),
            jax.ShapeDtypeStruct((col.shape[0], 128), f32),
            jax.ShapeDtypeStruct((8, 128), f32),
        ],
        compiler_params=pltpu.CompilerParams(vmem_limit_bytes=VMEM_LIMIT),
        name="hidden_back",
    )(*args)


def end_kernel(
    info_ref, own_ref, other_ref, gath_ref, link_ref, last_ref,
    one_ref, pool_ref, pair_ref, bias_ref, mean_ref, out_link_ref,
    red, mean_all, col_all, *, scale, count, stride,
):
    core = info_ref[0]
    red[pl.ds(pl.multiple_of(core * HALF, 8), HALF), :] = own_ref[...]
    red[pl.ds(pl.multiple_of((1 - core) * HALF, 8), HALF), :] = other_ref[...]
    one_ref[...] = scale * red[0:256, :]
    pool_ref[...] = scale * red[256:288, :]
    pair_ref[...] = (scale / 256.0) * red[288:320, 0:128].T[0:32, :]
    bias_ref[...] = (scale / 256.0) * red[320:321, 0:32]
    devices = gath_ref.shape[0] // stride
    for d in range(devices):
        mean_all[d * count : (d + 1) * count, :] = gath_ref[d * stride : d * stride + count, :]
        base = d * stride + count
        col_all[d * count : (d + 1) * count, :] = gath_ref[base : base + count, :]
    mean_ref[...] = scale * dot(mean_all[...], col_all[...], 0, 0, HIGH)
    out_link_ref[...] = link_ref[...]
    at = pl.multiple_of(info_ref[1] * stride + 2 * count, 8)
    jump = gath_ref[pl.ds(at, 8), 0:128] + last_ref[...]
    total = jnp.sum(jump * jump, axis=0, keepdims=True) * (1.0 / (12.0 * step_tau))
    out_link_ref[count - 1 : count, :] = jnp.where(info_ref[2] == 1, 0.0, total)


def end_call(info, own, other, gath, link, last, scale, count, stride):
    whole = pl.BlockSpec(memory_space=pltpu.VMEM)
    args = (info, own, other, gath, link, last)
    devices = gath.shape[0] // stride

    def body(*refs):
        end_kernel(*refs, scale=scale, count=count, stride=stride)

    return pl.pallas_call(
        body,
        in_specs=[pl.BlockSpec(memory_space=pltpu.SMEM)] + [whole] * (len(args) - 1),
        out_specs=[whole] * 6,
        out_shape=[
            jax.ShapeDtypeStruct((256, 256), f32),
            jax.ShapeDtypeStruct((32, 256), f32),
            jax.ShapeDtypeStruct((32, 32), f32),
            jax.ShapeDtypeStruct((1, 32), f32),
            jax.ShapeDtypeStruct((256, 256), f32),
            jax.ShapeDtypeStruct((count, 128), f32),
        ],
        scratch_shapes=[
            pltpu.VMEM((RED, 256), f32),
            pltpu.VMEM((devices * count, 256), f32),
            pltpu.VMEM((devices * count, 256), f32),
        ],
        compiler_params=pltpu.CompilerParams(vmem_limit_bytes=VMEM_LIMIT),
        name="unpack",
    )(*args)


def local(
    positions, hidden, cotangent, embed_weight, embed_bias, pair_weight, pair_bias,
    one_weight, pool_weight, mean_weight, one_bias, drift_weight,
):
    count, own_count, width = hidden.shape
    slices = lax.axis_size("slices")
    bits = slices.bit_length() - 1
    scale = 1.0 / math.sqrt(count * slices * own_count * lax.axis_size("ering"))
    core = lax.axis_index("ering")
    place = lax.axis_index("slices")

    def swap(array):
        return lax.ppermute(array, "ering", [(0, 1), (1, 0)])

    other_pos = swap(positions)
    part_sum = jnp.sum(hidden.astype(f32), axis=1)
    other_sum = swap(part_sum)
    pooled, h_sums, g_sums = pair_call(
        positions, other_pos, embed_weight, embed_bias, pair_weight, pair_bias
    )
    flat = (count * own_count, width)
    hid = hidden.reshape(flat)
    cot = cotangent.reshape(flat)
    core_arr = core.reshape(1).astype(jnp.int32)
    updated, pre, keep, send, mean_rows = one_call(
        core_arr, hid, cot, pooled.reshape(flat), h_sums.reshape(-1, 256),
        g_sums.reshape(-1, 256), part_sum, other_sum, one_weight, pool_weight, mean_weight, one_bias,
    )
    came = swap(send)
    total = keep + came[:HALF]
    col_total = send[HALF:] + came[HALF:]
    border = jnp.pad(positions[:, 0, :], ((0, 5), (0, 128)))
    gath = jnp.concatenate([mean_rows, col_total, border], axis=0)
    stride = gath.shape[0]
    hidden_grad, link, last = back_call(
        cot, pre, updated, col_total, positions, one_weight, mean_weight, drift_weight
    )
    orders = [[(t + e) % max(bits, 1) for t in range(bits)] for e in range(2)]
    for t in range(bits):
        pairs = [
            (s * 2 + e, (s ^ (1 << orders[e][t])) * 2 + e) for s in range(slices) for e in range(2)
        ]
        came = lax.ppermute(
            jnp.concatenate([total, gath], axis=0), ("slices", "ering"), pairs
        )
        total = total + came[:HALF]
        gath = jnp.concatenate([gath, came[HALF:]], axis=0)
    other_total = swap(total)
    apart = place ^ jnp.minimum(place + 1, slices - 1)
    found = jnp.int32(0)
    for t in range(bits):
        bit = jnp.where(core == 0, apart >> orders[0][t], apart >> orders[1][t]) & 1
        found = found + (bit << t)
    info = jnp.stack([core, found, (place == slices - 1).astype(jnp.int32)]).astype(jnp.int32)
    one_grad, pool_grad, pair_grad, bias_grad, mean_grad, link_terms = end_call(
        info, total, other_total, gath, link, last, scale, count, stride
    )
    return (
        updated.reshape(hidden.shape),
        hidden_grad.reshape(hidden.shape),
        link_terms,
        pair_grad,
        bias_grad.reshape(-1),
        one_grad,
        pool_grad,
        mean_grad,
    )


def solution(mesh):
    in_specs = (
        P(None, ("groups", "slices"), "ering"),
        P(("groups", "slices"), "ering", None),
        P(("groups", "slices"), "ering", None),
    ) + (P(),) * 9
    out_specs = (
        P(("groups", "slices"), "ering", None),
        P(("groups", "slices"), "ering", None),
        P(("groups", "slices"), "ering"),
        P("groups", None),
        P("groups"),
        P("groups", None),
        P("groups", None),
        P("groups", None),
    )
    return jax.shard_map(local, mesh=mesh, in_specs=in_specs, out_specs=out_specs, check_vma=False)
```

```python
import math

import jax
import jax.numpy as jnp
from jax import lax
from jax.experimental import pallas as pl
from jax.experimental.pallas import tpu as pltpu
from jax.sharding import PartitionSpec as P

HIGH = lax.Precision.HIGHEST
f32 = jnp.float32
bf16 = jnp.bfloat16
step_tau = 0.5
VMEM_LIMIT = 56 << 20
ONE, POOL, SMALL = 128, 16, 8
HALF = ONE + POOL + SMALL
SENT = HALF + SMALL
GATH = 24
PARAMS = pltpu.CompilerParams(vmem_limit_bytes=VMEM_LIMIT)
VMEM = pl.BlockSpec(memory_space=pltpu.VMEM)
SMEM = pl.BlockSpec(memory_space=pltpu.SMEM)


def dot(a, b, ca, cb, precision=None):
    return lax.dot_general(
        a, b, (((ca,), (cb,)), ((), ())), preferred_element_type=f32, precision=precision
    )


def split3(x):
    first = x.astype(bf16).astype(f32)
    rest = x - first
    second = rest.astype(bf16).astype(f32)
    return first, second, rest - second


def iota(shape, dim):
    return lax.broadcasted_iota(jnp.int32, shape, dim)


def main_kernel(
    core_ref, own_ref, other_ref, ew_ref, eb_ref, pw_ref, pb_ref, hid_ref, cot_ref,
    sum_a_ref, sum_b_ref, ow_ref, qw_ref, mw_ref, ob_ref,
    updated_ref, grad_ref, keep_ref, send_ref, mean_ref,
    embed_mat, block_mat, a_rows, feat, bias_row, pool_mat, columns,
    pre_a, pre_b, act_a, act_b, in_buf, slope_a, slope_b, sum_buf,
    pooled_all, h_all, g_all, hid_all, cot_all, one_pre, back_all,
):
    s = pl.program_id(0)
    count = own_ref.shape[1]

    def features(slot, at, first, size):
        lane = iota((size, 128), 1)
        square = jnp.ones((size, 128), f32)
        misc = jnp.zeros((size, 128), f32)
        for c in range(3):
            spread = jnp.broadcast_to(
                columns[at, first : first + size, c : c + 1], (size, 128)
            )
            offset = spread - own_ref[c, pl.ds(at, 1), :]
            square = square + offset * offset
            s1, s2, s3 = split3(spread)
            base = 64 + 6 * c
            misc = jnp.where((lane >= base) & (lane < base + 3), s1, misc)
            misc = jnp.where((lane >= base + 3) & (lane < base + 5), s2, misc)
            misc = jnp.where(lane == base + 5, s3, misc)
        radial = jnp.sqrt(square)
        high = radial.astype(bf16).astype(f32)
        low = radial - high
        high_turned = pltpu.roll(high, 64, 1)
        low_turned = pltpu.roll(low, 64, 1)
        left = lane < 64
        rows = slice(first, first + size)
        feat[slot, 0, rows, :128] = jnp.where(left, high, low_turned).astype(bf16)
        feat[slot, 0, rows, 128:] = jnp.where(left, high, misc).astype(bf16)
        feat[slot, 1, rows, :128] = jnp.where(left, high_turned, low).astype(bf16)
        feat[slot, 1, rows, 128:] = jnp.where(left, high_turned, misc).astype(bf16)

    @pl.when(s == 0)
    def _():
        wide = jnp.concatenate([ew_ref[...]] * 8, axis=1)
        w1, w2, w3 = split3(wide)
        row = iota((64, 256), 0)
        lane = iota((64, 256), 1)
        pieces = (w1, w2, w3, w1, w2, w1)
        misc = jnp.zeros((64, 256), f32)
        for c in range(3):
            for p in range(6):
                misc = jnp.where(row == 6 * c + p, -pieces[p][c : c + 1, :], misc)
        misc = misc.astype(bf16)
        for g in range(8):
            hit = row == g * 8 + lane // 32
            first = jnp.where(hit, w1[3:4, :], 0.0).astype(bf16)
            embed_mat[0:64, g * 256 : (g + 1) * 256] = first
            embed_mat[64:128, g * 256 : (g + 1) * 256] = first
            embed_mat[128:192, g * 256 : (g + 1) * 256] = jnp.where(hit, w2[3:4, :], 0.0).astype(bf16)
            embed_mat[192:256, g * 256 : (g + 1) * 256] = misc
        row = iota((256, 256), 0)
        lane = iota((256, 256), 1)
        tiled = jnp.concatenate([pw_ref[...].astype(f32).T] * 8, axis=1)
        tiled = jnp.concatenate([tiled] * 8, axis=0)
        block_mat[...] = jnp.where(row // 32 == lane // 32, tiled, 0.0).astype(bf16)
        pool_mat[...] = jnp.concatenate([qw_ref[...]] * 8, axis=0)
        bias_row[...] = jnp.broadcast_to(jnp.concatenate([pb_ref[...]] * 8, axis=1), (8, 256))
        wide_bias = jnp.concatenate([eb_ref[...]] * 8, axis=1)
        electron = iota((128, 256), 0)
        lane128 = iota((128, 256), 1)
        points = jnp.concatenate(
            [piece for c in range(3) for piece in split3(own_ref[c])], axis=0
        ).astype(bf16)
        for g in range(16):
            pick = jnp.where(electron == g * 8 + lane128 // 32, 1.0, 0.0).astype(bf16)
            spread = dot(points, pick, 1, 0)
            total = jnp.broadcast_to(wide_bias, (count, 256))
            for c in range(3):
                base = 3 * c * count
                point = (
                    spread[base : base + count]
                    + spread[base + count : base + 2 * count]
                    + spread[base + 2 * count : base + 3 * count]
                )
                total = total + point * wide[c : c + 1, :]
            a_rows[:, g * 256 : (g + 1) * 256] = total
        blank = jnp.zeros((5, 256), f32)
        for at in range(count):
            stacked = jnp.concatenate(
                [
                    jnp.concatenate(
                        [own_ref[c, at : at + 1, :], other_ref[c, at : at + 1, :]], axis=1
                    )
                    for c in range(3)
                ]
                + [blank],
                axis=0,
            )
            columns[at] = stacked.T
        features(0, 0, 0, 256)

    @pl.when(s < count)
    def _():
        diagonal = iota((8, 256), 0) == iota((8, 256), 1) // 32
        block = iota((32, 256), 1) // 32
        slot = lax.rem(s, 2)
        later = jnp.minimum(s + 1, count - 1)
        hid = hid_ref[0]
        pre = (pre_a, pre_b)
        acts = (act_a, act_b)
        slopes = (slope_a, slope_b)

        def embed(g):
            half, inner = g // 8, g % 8
            out = dot(feat[slot, half], embed_mat[:, inner * 256 : (inner + 1) * 256], 1, 0)
            pre[g % 2][...] = out + a_rows[pl.ds(s, 1), g * 256 : (g + 1) * 256]
            features(1 - slot, later, g * 16, 16)

        def first_tanh(g):
            out = jnp.tanh(pre[g % 2][...])
            in_buf[g % 4] = out.astype(bf16)
            sum_buf[g % 4] = jnp.sum(out.reshape(32, 8, 256), axis=0)

        def layer(g):
            acts[g % 2][...] = dot(in_buf[g % 4], block_mat[...], 1, 0) + bias_row[0:1, :]

        def second_tanh(g):
            act = jnp.tanh(acts[g % 2][...])
            total = sum_buf[g % 4] + jnp.sum(act.reshape(32, 8, 256), axis=0)
            mean = jnp.sum(total, axis=0, keepdims=True) * (1.0 / 256)
            slope = 1.0 - act * act
            h_all[s, g : g + 1, :] = jnp.sum(slope, axis=0, keepdims=True)
            pooled_all[s, g * 8 : (g + 1) * 8, :] = jnp.where(diagonal, mean, 0.0)
            slopes[g % 2][...] = slope.astype(bf16)

        def outer(g):
            product = dot(in_buf[g % 4], slopes[g % 2][...], 0, 0)
            picked = product[0:32]
            for q in range(1, 8):
                picked = jnp.where(block == q, product[q * 32 : (q + 1) * 32], picked)
            g_all[s, g * 32 : (g + 1) * 32, :] = picked

        for step in range(16 + 4):
            for lag, stage in enumerate((embed, first_tanh, layer, second_tanh, outer)):
                if 0 <= step - lag < 16:
                    stage(step - lag)
        hid_all[s] = hid
        cot_all[s] = cot_ref[0]
        one_pre[s] = dot(hid, ow_ref[...], 1, 0)

    @pl.when(s == count)
    def _():
        mean_rows = ((sum_a_ref[...] + sum_b_ref[...]) * (1.0 / 256)).astype(bf16)
        mean_ref[...] = mean_rows
        per_slice = dot(mean_rows, mw_ref[...], 1, 0) + ob_ref[...]
        own_lanes = iota((128, 256), 0) % 8 == iota((128, 256), 1) // 32
        one_total = jnp.zeros((256, 256), f32)
        pool_total = jnp.zeros((256, 256), f32)
        pair_total = jnp.zeros((32, 256), f32)
        bias_total = jnp.zeros((16, 256), f32)
        parts = []
        for step in range(count + 2):
            if step < count:
                at = step
                rows = slice(at * 128, (at + 1) * 128)
                pre = one_pre[at] + dot(pooled_all[at].astype(bf16), pool_mat[...], 1, 0)
                act = jnp.tanh(pre + per_slice[at : at + 1, :])
                updated_ref[rows, :] = (act + hid_all[at].astype(f32)).astype(bf16)
                grad = (cot_all[at].astype(f32) * (1.0 - act * act)).astype(bf16)
                grad_ref[rows, :] = grad
                parts.append(jnp.sum(grad.astype(f32), axis=0, keepdims=True))
            if 0 <= step - 1 < count:
                at = step - 1
                grad = grad_ref[at * 128 : (at + 1) * 128, :]
                back = jnp.where(own_lanes, dot(grad, pool_mat[...], 1, 1), 0.0)
                back_all[at] = jnp.sum(back.reshape(16, 8, 256), axis=1)
                one_total = one_total + dot(hid_all[at], grad, 0, 0)
                pool_total = pool_total + dot(pooled_all[at].astype(bf16), grad, 0, 0)
            if 0 <= step - 2 < count:
                at = step - 2
                bias_total = bias_total + back_all[at] * h_all[at]
                for g in range(16):
                    pair_total = pair_total + g_all[at, g * 32 : (g + 1) * 32, :] * back_all[at, g : g + 1, :]
        fold = jnp.where(iota((256, 256), 0) % 32 == iota((256, 256), 1) % 32, 1.0, 0.0)
        pool = pool_total[0:32]
        for q in range(1, 8):
            pool = pool + pool_total[q * 32 : (q + 1) * 32]
        bias_one = jnp.broadcast_to(jnp.sum(bias_total, axis=0, keepdims=True), (8, 256))
        folded = dot(jnp.concatenate([pair_total, bias_one], axis=0), fold, 1, 0, HIGH)
        picked = jnp.where(iota((32, 256), 0) % 8 == iota((32, 256), 1) // 32, folded[0:32], 0.0)
        packed = jnp.sum(picked.reshape(4, 8, 256), axis=1)
        small = jnp.concatenate([packed, folded[32:36]], axis=0)
        core = core_ref[0]

        @pl.when(core == 0)
        def _():
            keep_ref[0:ONE, :] = one_total[0:ONE]
            send_ref[0:ONE, :] = one_total[ONE:]
            keep_ref[ONE : ONE + POOL, :] = pool[0:POOL]
            send_ref[ONE : ONE + POOL, :] = pool[POOL:]

        @pl.when(core == 1)
        def _():
            send_ref[0:ONE, :] = one_total[0:ONE]
            keep_ref[0:ONE, :] = one_total[ONE:]
            send_ref[ONE : ONE + POOL, :] = pool[0:POOL]
            keep_ref[ONE : ONE + POOL, :] = pool[POOL:]

        keep_ref[ONE + POOL : HALF, :] = small
        send_ref[ONE + POOL : HALF, :] = small
        sums = jnp.concatenate(parts, axis=0)
        keep_ref[HALF:, :] = sums
        send_ref[HALF:, :] = sums


def main_call(core, own, other, ew, eb, pw, pb, hid, cot, sum_a, sum_b, ow, qw, mw, ob):
    count, rows, width = hid.shape
    args = (
        core, own, other, ew.T, eb.reshape(1, 32), pw, pb.reshape(1, 32), hid, cot,
        sum_a, sum_b, ow, qw, mw, ob.reshape(1, width),
    )
    whole = [pl.BlockSpec(a.shape, lambda s, n=a.ndim: (0,) * n) for a in args]
    by_slice = pl.BlockSpec((1, rows, width), lambda s: (jnp.minimum(s, count - 1), 0, 0))
    in_specs = [SMEM] + whole[1:7] + [by_slice, by_slice] + whole[9:]
    shapes = [
        jax.ShapeDtypeStruct((count * rows, width), bf16),
        jax.ShapeDtypeStruct((count * rows, width), bf16),
        jax.ShapeDtypeStruct((HALF + count, width), f32),
        jax.ShapeDtypeStruct((HALF + count, width), f32),
        jax.ShapeDtypeStruct((count, width), bf16),
    ]
    return pl.pallas_call(
        main_kernel,
        grid=(count + 1,),
        in_specs=in_specs,
        out_specs=[pl.BlockSpec(a.shape, lambda s: (0, 0)) for a in shapes],
        out_shape=shapes,
        scratch_shapes=[
            pltpu.VMEM((256, 2048), bf16),
            pltpu.VMEM((256, 256), bf16),
            pltpu.VMEM((count, 4096), f32),
            pltpu.VMEM((2, 2, 256, 256), bf16),
            pltpu.VMEM((8, 256), f32),
            pltpu.VMEM((256, 256), bf16),
            pltpu.VMEM((count, 256, 8), f32),
            pltpu.VMEM((256, 256), f32),
            pltpu.VMEM((256, 256), f32),
            pltpu.VMEM((256, 256), f32),
            pltpu.VMEM((256, 256), f32),
            pltpu.VMEM((4, 256, 256), bf16),
            pltpu.VMEM((256, 256), bf16),
            pltpu.VMEM((256, 256), bf16),
            pltpu.VMEM((4, 8, 256), f32),
            pltpu.VMEM((count, 128, 256), f32),
            pltpu.VMEM((count, 16, 256), f32),
            pltpu.VMEM((count, 512, 256), f32),
            pltpu.VMEM((count, 128, 256), bf16),
            pltpu.VMEM((count, 128, 256), bf16),
            pltpu.VMEM((count, 128, 256), f32),
            pltpu.VMEM((count, 16, 256), f32),
        ],
        compiler_params=PARAMS,
        name="pair_and_one",
    )(*args)


def pack(total, gath, out_ref):
    out_ref[0:HALF, :] = total.astype(bf16)
    small = total[ONE + POOL :]
    out_ref[HALF:SENT, :] = (small - small.astype(bf16).astype(f32)).astype(bf16)
    at = SENT
    for piece in gath:
        out_ref[at : at + piece.shape[0], :] = piece
        at += piece.shape[0]


def first_kernel(keep_ref, came_ref, mean_ref, pos_ref, out_ref, col_ref):
    both = keep_ref[...] + came_ref[...]
    col = both[HALF:]
    col_ref[...] = col
    p1, p2, p3 = split3(pos_ref[:, 0, :])
    blank = jnp.zeros((2, 256), f32)
    border = jnp.concatenate(
        [
            jnp.concatenate([p1, p2], axis=1),
            jnp.concatenate([p3, jnp.zeros_like(p3)], axis=1),
            blank,
        ],
        axis=0,
    )
    gath = jnp.concatenate([mean_ref[...].astype(f32), col, border], axis=0).astype(bf16)
    pack(both[0:HALF], [gath], out_ref)


def first_call(keep, came, mean_rows, pos):
    count = mean_rows.shape[0]
    return pl.pallas_call(
        first_kernel,
        in_specs=[VMEM] * 4,
        out_specs=[VMEM] * 2,
        out_shape=[
            jax.ShapeDtypeStruct((SENT + 2 * count + 8, 256), bf16),
            jax.ShapeDtypeStruct((count, 256), f32),
        ],
        compiler_params=PARAMS,
        name="first_mix",
    )(keep, came, mean_rows, pos)


def add_up(own_ref, came_ref):
    total = own_ref[0:HALF, :].astype(f32) + came_ref[0:HALF, :].astype(f32)
    rest = own_ref[HALF:SENT, :].astype(f32) + came_ref[HALF:SENT, :].astype(f32)
    return jnp.concatenate([total[0 : ONE + POOL], total[ONE + POOL :] + rest], axis=0)


def mix_kernel(own_ref, came_ref, out_ref):
    pack(add_up(own_ref, came_ref), [own_ref[SENT:, :], came_ref[SENT:, :]], out_ref)


def mix_call(own, came):
    rows = SENT + 2 * (own.shape[0] - SENT)
    return pl.pallas_call(
        mix_kernel,
        in_specs=[VMEM] * 2,
        out_specs=VMEM,
        out_shape=jax.ShapeDtypeStruct((rows, 256), bf16),
        compiler_params=PARAMS,
        name="mix",
    )(own, came)


def last_kernel(own_ref, came_ref, out_ref):
    out_ref[...] = add_up(own_ref, came_ref)


def last_call(own, came):
    return pl.pallas_call(
        last_kernel,
        in_specs=[VMEM] * 2,
        out_specs=VMEM,
        out_shape=jax.ShapeDtypeStruct((HALF, 256), f32),
        compiler_params=PARAMS,
        name="last_mix",
    )(own, came)


def back_kernel(
    cot_ref, pre_ref, upd_ref, col_ref, pos_ref, ow_ref, mw_ref, dw_ref,
    grad_ref, link_ref, last_ref,
):
    count = col_ref.shape[0]
    back = dot(col_ref[...], mw_ref[...].astype(f32), 1, 1, HIGH) * (1.0 / 256)
    drifts = []
    for s in range(count):
        at = slice(s * 128, (s + 1) * 128)
        grad = cot_ref[at, :].astype(f32) + dot(pre_ref[at, :], ow_ref[...], 1, 1)
        grad_ref[at, :] = (grad + back[s : s + 1, :]).astype(bf16)
        drifts.append(dot(dw_ref[...], upd_ref[at, :], 1, 1))
    for s in range(count):
        here = [-pos_ref[c, s : s + 1, :] - step_tau * drifts[s][c : c + 1, :] for c in range(3)]
        if s < count - 1:
            jumps = [here[c] + pos_ref[c, s + 1 : s + 2, :] for c in range(3)]
            total = jumps[0] * jumps[0] + jumps[1] * jumps[1] + jumps[2] * jumps[2]
            link_ref[s : s + 1, :] = total * (1.0 / (12.0 * step_tau))
        else:
            link_ref[s : s + 1, :] = jnp.zeros((1, 128), f32)
            last_ref[...] = jnp.concatenate(here + [jnp.zeros((5, 128), f32)], axis=0)


def back_call(cot, pre, updated, col, pos, ow, mw, dw):
    args = (cot, pre, updated, col, pos, ow, mw, dw)
    return pl.pallas_call(
        back_kernel,
        in_specs=[VMEM] * len(args),
        out_specs=[VMEM] * 3,
        out_shape=[
            jax.ShapeDtypeStruct(cot.shape, bf16),
            jax.ShapeDtypeStruct((col.shape[0], 128), f32),
            jax.ShapeDtypeStruct((8, 128), f32),
        ],
        compiler_params=PARAMS,
        name="hidden_back",
    )(*args)


def mean_kernel(
    info_ref, own_ref, came_ref, link_ref, last_ref,
    mean_ref, out_link_ref,
    mean_all, col_all, border, *, scale, count,
):
    stride = 2 * count + 8
    half = (own_ref.shape[0] - SENT) // stride
    for d in range(2 * half):
        ref = own_ref if d < half else came_ref
        base = SENT + (d % half) * stride
        block = ref[base : base + stride, :].astype(f32)
        at = pl.ds(pl.multiple_of(info_ref[2 + d] * count, 8), count)
        mean_all[at, :] = block[0:count]
        col_all[at, :] = block[count : 2 * count]
        border[pl.ds(pl.multiple_of(info_ref[2 + d] * 8, 8), 8), :] = block[2 * count :]
    mean_ref[...] = scale * dot(mean_all[...].astype(bf16), col_all[...].astype(bf16), 0, 0)
    out_link_ref[...] = link_ref[...]
    pieces = border[pl.ds(pl.multiple_of(info_ref[0] * 8, 8), 8), :]
    point = pieces[0:3, 0:128] + pieces[0:3, 128:] + pieces[3:6, 0:128]
    jump = point + last_ref[0:3, :]
    total = jnp.sum(jump * jump, axis=0, keepdims=True) * (1.0 / (12.0 * step_tau))
    out_link_ref[count - 1 : count, :] = jnp.where(info_ref[1] == 1, 0.0, total)


def mean_call(info, own, came, link, last, scale, count):
    args = (info, own, came, link, last)
    devices = info.shape[0] - 2

    def body(*refs):
        mean_kernel(*refs, scale=scale, count=count)

    return pl.pallas_call(
        body,
        in_specs=[SMEM] + [VMEM] * 4,
        out_specs=[VMEM] * 2,
        out_shape=[
            jax.ShapeDtypeStruct((256, 256), f32),
            jax.ShapeDtypeStruct((count, 128), f32),
        ],
        scratch_shapes=[
            pltpu.VMEM((devices * count, 256), f32),
            pltpu.VMEM((devices * count, 256), f32),
            pltpu.VMEM((devices * 8, 256), f32),
        ],
        compiler_params=PARAMS,
        name="mean_and_link",
    )(*args)


def end_kernel(core_ref, own_ref, came_ref, one_ref, pool_ref, pair_ref, bias_ref, *, scale):
    def write(low_ref, high_ref):
        one_ref[0:ONE, :] = scale * low_ref[0:ONE, :]
        one_ref[ONE:, :] = scale * high_ref[0:ONE, :]
        pool_ref[0:POOL, :] = scale * low_ref[ONE : ONE + POOL, :]
        pool_ref[POOL:, :] = scale * high_ref[ONE : ONE + POOL, :]

        small = low_ref[ONE + POOL : HALF, :]
        rows = jnp.concatenate(
            [jnp.broadcast_to(small[r : r + 1], (8, 256)) for r in range(4)], axis=0
        )
        rows = jnp.where(iota((32, 256), 0) % 8 == iota((32, 256), 1) // 32, rows, 0.0)
        total = rows[:, 0:128] + rows[:, 128:]
        total = total + pltpu.roll(total, 64, 1)
        total = total + pltpu.roll(total, 32, 1)
        pair_ref[...] = (scale / 256.0) * total[:, 0:32].T
        bias_ref[...] = (scale / 256.0) * small[4:5, 0:32]

    core = core_ref[0]
    pl.when(core == 0)(lambda: write(own_ref, came_ref))
    pl.when(core == 1)(lambda: write(came_ref, own_ref))


def end_call(core, own, came, scale):
    def body(*refs):
        end_kernel(*refs, scale=scale)

    return pl.pallas_call(
        body,
        in_specs=[SMEM, VMEM, VMEM],
        out_specs=[VMEM] * 4,
        out_shape=[
            jax.ShapeDtypeStruct((256, 256), f32),
            jax.ShapeDtypeStruct((32, 256), f32),
            jax.ShapeDtypeStruct((32, 32), f32),
            jax.ShapeDtypeStruct((1, 32), f32),
        ],
        compiler_params=PARAMS,
        name="unpack",
    )(core, own, came)


def local(
    positions, hidden, cotangent, embed_weight, embed_bias, pair_weight, pair_bias,
    one_weight, pool_weight, mean_weight, one_bias, drift_weight,
):
    count, own_count, width = hidden.shape
    slices = lax.axis_size("slices")
    bits = slices.bit_length() - 1
    scale = 1.0 / math.sqrt(count * slices * own_count * lax.axis_size("ering"))
    core = lax.axis_index("ering").astype(jnp.int32)
    place = lax.axis_index("slices").astype(jnp.int32)

    def swap(array):
        return lax.ppermute(array, "ering", [(0, 1), (1, 0)])

    orders = [[(t + e) % bits for t in range(bits)] for e in range(2)]
    masks = [
        [sum(((d >> t) & 1) << orders[e][t] for t in range(bits)) for d in range(slices)]
        for e in range(2)
    ]
    owners = place ^ jnp.where(core == 0, jnp.array(masks[0]), jnp.array(masks[1]))
    info = jnp.concatenate(
        [
            jnp.minimum(place + 1, slices - 1).reshape(1),
            (place == slices - 1).astype(jnp.int32).reshape(1),
            owners.astype(jnp.int32),
        ]
    )
    core = core.reshape(1)

    other_pos = swap(positions)
    part_sum = jnp.sum(hidden.astype(f32), axis=1)
    other_sum = swap(part_sum)
    updated, pre, keep, send, mean_rows = main_call(
        core, positions, other_pos, embed_weight, embed_bias, pair_weight, pair_bias, hidden,
        cotangent, part_sum, other_sum, one_weight, pool_weight, mean_weight, one_bias,
    )
    state, col_total = first_call(keep, swap(send), mean_rows, positions)
    hidden_grad, link, last = back_call(
        cotangent.reshape(pre.shape), pre, updated, col_total, positions, one_weight,
        mean_weight, drift_weight,
    )
    for t in range(bits):
        pairs = [
            (s * 2 + e, (s ^ (1 << orders[e][t])) * 2 + e) for s in range(slices) for e in range(2)
        ]
        came = lax.ppermute(state, ("slices", "ering"), pairs)
        if t < bits - 1:
            state = mix_call(state, came)
    total = last_call(state, came)
    other_total = swap(total)
    mean_grad, link_terms = mean_call(info, state, came, link, last, scale, count)
    one_grad, pool_grad, pair_grad, bias_grad = end_call(core, total, other_total, scale)
    return (
        updated.reshape(hidden.shape),
        hidden_grad.reshape(hidden.shape),
        link_terms,
        pair_grad,
        bias_grad.reshape(-1),
        one_grad,
        pool_grad,
        mean_grad,
    )


def solution(mesh):
    in_specs = (
        P(None, ("groups", "slices"), "ering"),
        P(("groups", "slices"), "ering", None),
        P(("groups", "slices"), "ering", None),
    ) + (P(),) * 9
    out_specs = (
        P(("groups", "slices"), "ering", None),
        P(("groups", "slices"), "ering", None),
        P(("groups", "slices"), "ering"),
        P("groups", None),
        P("groups"),
        P("groups", None),
        P("groups", None),
        P("groups", None),
    )
    return jax.shard_map(local, mesh=mesh, in_specs=in_specs, out_specs=out_specs, check_vma=False)
```

```python
import math

import jax
import jax.numpy as jnp
from jax import lax
from jax.experimental import pallas as pl
from jax.experimental.pallas import tpu as pltpu
from jax.sharding import PartitionSpec as P

HIGH = lax.Precision.HIGHEST
f32 = jnp.float32
bf16 = jnp.bfloat16
step_tau = 0.5
ONE, POOL, SMALL = 128, 16, 8
HALF = ONE + POOL + SMALL
SENT = HALF + SMALL
GATH = 24
PARAMS = pltpu.CompilerParams(vmem_limit_bytes=16 << 20)
VMEM = pl.BlockSpec(memory_space=pltpu.VMEM)
SMEM = pl.BlockSpec(memory_space=pltpu.SMEM)


def near(array):
    return pltpu.with_memory_space_constraint(array, pltpu.VMEM)


def far(array):
    return pltpu.with_memory_space_constraint(array, pltpu.HBM)


def dot(a, b, ca, cb, precision=None):
    return lax.dot_general(
        a, b, (((ca,), (cb,)), ((), ())), preferred_element_type=f32, precision=precision
    )


def split3(x):
    first = x.astype(bf16).astype(f32)
    rest = x - first
    second = rest.astype(bf16).astype(f32)
    return first, second, rest - second


def iota(shape, dim):
    return lax.broadcasted_iota(jnp.int32, shape, dim)


def main_kernel(
    core_ref, own_ref, other_ref, ew_ref, eb_ref, pw_ref, pb_ref, hid_ref, cot_ref,
    sum_a_ref, sum_b_ref, ow_ref, qw_ref, mw_ref, ob_ref,
    updated_ref, grad_ref, keep_ref, send_ref, mean_ref,
    embed_mat, block_mat, a_rows, feat, bias_row, pool_mat, columns,
    pre_a, pre_b, act_a, act_b, in_buf, slope_a, slope_b, sum_buf,
    pooled_all, h_all, g_all, hid_all, cot_all, one_pre, back_all,
):
    s = pl.program_id(0)
    count = own_ref.shape[1]

    def features(slot, at, first, size):
        lane = iota((size, 128), 1)
        square = jnp.ones((size, 128), f32)
        misc = jnp.zeros((size, 128), f32)
        for c in range(3):
            spread = jnp.broadcast_to(
                columns[at, first : first + size, c : c + 1], (size, 128)
            )
            offset = spread - own_ref[c, pl.ds(at, 1), :]
            square = square + offset * offset
            s1, s2, s3 = split3(spread)
            base = 64 + 6 * c
            misc = jnp.where((lane >= base) & (lane < base + 3), s1, misc)
            misc = jnp.where((lane >= base + 3) & (lane < base + 5), s2, misc)
            misc = jnp.where(lane == base + 5, s3, misc)
        radial = jnp.sqrt(square)
        high = radial.astype(bf16).astype(f32)
        low = radial - high
        high_turned = pltpu.roll(high, 64, 1)
        low_turned = pltpu.roll(low, 64, 1)
        left = lane < 64
        rows = slice(first, first + size)
        feat[slot, 0, rows, :128] = jnp.where(left, high, low_turned).astype(bf16)
        feat[slot, 0, rows, 128:] = jnp.where(left, high, misc).astype(bf16)
        feat[slot, 1, rows, :128] = jnp.where(left, high_turned, low).astype(bf16)
        feat[slot, 1, rows, 128:] = jnp.where(left, high_turned, misc).astype(bf16)

    @pl.when(s == 0)
    def _():
        wide = jnp.concatenate([ew_ref[...]] * 8, axis=1)
        w1, w2, w3 = split3(wide)
        row = iota((64, 256), 0)
        lane = iota((64, 256), 1)
        pieces = (w1, w2, w3, w1, w2, w1)
        misc = jnp.zeros((64, 256), f32)
        for c in range(3):
            for p in range(6):
                misc = jnp.where(row == 6 * c + p, -pieces[p][c : c + 1, :], misc)
        misc = misc.astype(bf16)
        for g in range(8):
            hit = row == g * 8 + lane // 32
            first = jnp.where(hit, w1[3:4, :], 0.0).astype(bf16)
            embed_mat[0:64, g * 256 : (g + 1) * 256] = first
            embed_mat[64:128, g * 256 : (g + 1) * 256] = first
            embed_mat[128:192, g * 256 : (g + 1) * 256] = jnp.where(hit, w2[3:4, :], 0.0).astype(bf16)
            embed_mat[192:256, g * 256 : (g + 1) * 256] = misc
        row = iota((256, 256), 0)
        lane = iota((256, 256), 1)
        tiled = jnp.concatenate([pw_ref[...].astype(f32).T] * 8, axis=1)
        tiled = jnp.concatenate([tiled] * 8, axis=0)
        block_mat[...] = jnp.where(row // 32 == lane // 32, tiled, 0.0).astype(bf16)
        pool_mat[...] = jnp.concatenate([qw_ref[...]] * 8, axis=0)
        bias_row[...] = jnp.broadcast_to(jnp.concatenate([pb_ref[...]] * 8, axis=1), (8, 256))
        wide_bias = jnp.concatenate([eb_ref[...]] * 8, axis=1)
        electron = iota((128, 256), 0)
        lane128 = iota((128, 256), 1)
        points = jnp.concatenate(
            [piece for c in range(3) for piece in split3(own_ref[c])], axis=0
        ).astype(bf16)
        for g in range(16):
            pick = jnp.where(electron == g * 8 + lane128 // 32, 1.0, 0.0).astype(bf16)
            spread = dot(points, pick, 1, 0)
            total = jnp.broadcast_to(wide_bias, (count, 256))
            for c in range(3):
                base = 3 * c * count
                point = (
                    spread[base : base + count]
                    + spread[base + count : base + 2 * count]
                    + spread[base + 2 * count : base + 3 * count]
                )
                total = total + point * wide[c : c + 1, :]
            a_rows[:, g * 256 : (g + 1) * 256] = total
        blank = jnp.zeros((5, 256), f32)
        for at in range(count):
            stacked = jnp.concatenate(
                [
                    jnp.concatenate(
                        [own_ref[c, at : at + 1, :], other_ref[c, at : at + 1, :]], axis=1
                    )
                    for c in range(3)
                ]
                + [blank],
                axis=0,
            )
            columns[at] = stacked.T
        features(0, 0, 0, 256)

    @pl.when(s < count)
    def _():
        diagonal = iota((8, 256), 0) == iota((8, 256), 1) // 32
        block = iota((32, 256), 1) // 32
        slot = lax.rem(s, 2)
        later = jnp.minimum(s + 1, count - 1)
        hid = hid_ref[0]
        pre = (pre_a, pre_b)
        acts = (act_a, act_b)
        slopes = (slope_a, slope_b)

        def embed(g):
            half, inner = g // 8, g % 8
            out = dot(feat[slot, half], embed_mat[:, inner * 256 : (inner + 1) * 256], 1, 0)
            pre[g % 2][...] = out + a_rows[pl.ds(s, 1), g * 256 : (g + 1) * 256]
            features(1 - slot, later, g * 16, 16)

        def first_tanh(g):
            out = jnp.tanh(pre[g % 2][...])
            in_buf[g % 4] = out.astype(bf16)
            sum_buf[g % 4] = jnp.sum(out.reshape(32, 8, 256), axis=0)

        def layer(g):
            acts[g % 2][...] = dot(in_buf[g % 4], block_mat[...], 1, 0) + bias_row[0:1, :]

        def second_tanh(g):
            act = jnp.tanh(acts[g % 2][...])
            total = sum_buf[g % 4] + jnp.sum(act.reshape(32, 8, 256), axis=0)
            mean = jnp.sum(total, axis=0, keepdims=True) * (1.0 / 256)
            slope = 1.0 - act * act
            h_all[s, g : g + 1, :] = jnp.sum(slope, axis=0, keepdims=True)
            pooled_all[s, g * 8 : (g + 1) * 8, :] = jnp.where(diagonal, mean, 0.0)
            slopes[g % 2][...] = slope.astype(bf16)

        def outer(g):
            product = dot(in_buf[g % 4], slopes[g % 2][...], 0, 0)
            picked = product[0:32]
            for q in range(1, 8):
                picked = jnp.where(block == q, product[q * 32 : (q + 1) * 32], picked)
            g_all[s, g * 32 : (g + 1) * 32, :] = picked

        for step in range(16 + 4):
            for lag, stage in enumerate((embed, first_tanh, layer, second_tanh, outer)):
                if 0 <= step - lag < 16:
                    stage(step - lag)
        hid_all[s] = hid
        cot_all[s] = cot_ref[0]
        one_pre[s] = dot(hid, ow_ref[...], 1, 0)

    @pl.when(s == count)
    def _():
        mean_rows = ((sum_a_ref[...] + sum_b_ref[...]) * (1.0 / 256)).astype(bf16)
        mean_ref[...] = mean_rows
        per_slice = dot(mean_rows, mw_ref[...], 1, 0) + ob_ref[...]
        own_lanes = iota((128, 256), 0) % 8 == iota((128, 256), 1) // 32
        one_total = jnp.zeros((256, 256), f32)
        pool_total = jnp.zeros((256, 256), f32)
        pair_total = jnp.zeros((32, 256), f32)
        bias_total = jnp.zeros((16, 256), f32)
        parts = []
        for step in range(count + 2):
            if step < count:
                at = step
                rows = slice(at * 128, (at + 1) * 128)
                pre = one_pre[at] + dot(pooled_all[at].astype(bf16), pool_mat[...], 1, 0)
                act = jnp.tanh(pre + per_slice[at : at + 1, :])
                updated_ref[rows, :] = (act + hid_all[at].astype(f32)).astype(bf16)
                grad = (cot_all[at].astype(f32) * (1.0 - act * act)).astype(bf16)
                grad_ref[rows, :] = grad
                parts.append(jnp.sum(grad.astype(f32), axis=0, keepdims=True))
            if 0 <= step - 1 < count:
                at = step - 1
                grad = grad_ref[at * 128 : (at + 1) * 128, :]
                back = jnp.where(own_lanes, dot(grad, pool_mat[...], 1, 1), 0.0)
                back_all[at] = jnp.sum(back.reshape(16, 8, 256), axis=1)
                one_total = one_total + dot(hid_all[at], grad, 0, 0)
                pool_total = pool_total + dot(pooled_all[at].astype(bf16), grad, 0, 0)
            if 0 <= step - 2 < count:
                at = step - 2
                bias_total = bias_total + back_all[at] * h_all[at]
                for g in range(16):
                    pair_total = pair_total + g_all[at, g * 32 : (g + 1) * 32, :] * back_all[at, g : g + 1, :]
        fold = jnp.where(iota((256, 256), 0) % 32 == iota((256, 256), 1) % 32, 1.0, 0.0)
        pool = pool_total[0:32]
        for q in range(1, 8):
            pool = pool + pool_total[q * 32 : (q + 1) * 32]
        bias_one = jnp.broadcast_to(jnp.sum(bias_total, axis=0, keepdims=True), (8, 256))
        folded = dot(jnp.concatenate([pair_total, bias_one], axis=0), fold, 1, 0, HIGH)
        picked = jnp.where(iota((32, 256), 0) % 8 == iota((32, 256), 1) // 32, folded[0:32], 0.0)
        packed = jnp.sum(picked.reshape(4, 8, 256), axis=1)
        small = jnp.concatenate([packed, folded[32:36]], axis=0)
        core = core_ref[0]

        @pl.when(core == 0)
        def _():
            keep_ref[0:ONE, :] = one_total[0:ONE]
            send_ref[0:ONE, :] = one_total[ONE:]
            keep_ref[ONE : ONE + POOL, :] = pool[0:POOL]
            send_ref[ONE : ONE + POOL, :] = pool[POOL:]

        @pl.when(core == 1)
        def _():
            send_ref[0:ONE, :] = one_total[0:ONE]
            keep_ref[0:ONE, :] = one_total[ONE:]
            send_ref[ONE : ONE + POOL, :] = pool[0:POOL]
            keep_ref[ONE : ONE + POOL, :] = pool[POOL:]

        keep_ref[ONE + POOL : HALF, :] = small
        send_ref[ONE + POOL : HALF, :] = small
        sums = jnp.concatenate(parts, axis=0)
        keep_ref[HALF:, :] = sums
        send_ref[HALF:, :] = sums


def main_call(core, own, other, ew, eb, pw, pb, hid, cot, sum_a, sum_b, ow, qw, mw, ob):
    count, rows, width = hid.shape
    args = (
        core, far(own), near(other), far(ew.T), far(eb.reshape(1, 32)), far(pw),
        far(pb.reshape(1, 32)), far(hid), far(cot), near(sum_a), near(sum_b), far(ow), far(qw),
        far(mw), far(ob.reshape(1, width)),
    )
    by_slice = pl.BlockSpec((1, rows, width), lambda s: (jnp.minimum(s, count - 1), 0, 0))
    return pl.pallas_call(
        main_kernel,
        grid=(count + 1,),
        in_specs=[SMEM] + [VMEM] * 6 + [by_slice, by_slice] + [VMEM] * 6,
        out_specs=[VMEM] * 5,
        out_shape=[
            jax.ShapeDtypeStruct((count * rows, width), bf16),
            pltpu.VMEM((count * rows, width), bf16),
            pltpu.VMEM((HALF + count, width), f32),
            pltpu.VMEM((HALF + count, width), f32),
            pltpu.VMEM((count, width), bf16),
        ],
        scratch_shapes=[
            pltpu.VMEM((256, 2048), bf16),
            pltpu.VMEM((256, 256), bf16),
            pltpu.VMEM((count, 4096), f32),
            pltpu.VMEM((2, 2, 256, 256), bf16),
            pltpu.VMEM((8, 256), f32),
            pltpu.VMEM((256, 256), bf16),
            pltpu.VMEM((count, 256, 8), f32),
            pltpu.VMEM((256, 256), f32),
            pltpu.VMEM((256, 256), f32),
            pltpu.VMEM((256, 256), f32),
            pltpu.VMEM((256, 256), f32),
            pltpu.VMEM((4, 256, 256), bf16),
            pltpu.VMEM((256, 256), bf16),
            pltpu.VMEM((256, 256), bf16),
            pltpu.VMEM((4, 8, 256), f32),
            pltpu.VMEM((count, 128, 256), f32),
            pltpu.VMEM((count, 16, 256), f32),
            pltpu.VMEM((count, 512, 256), f32),
            pltpu.VMEM((count, 128, 256), bf16),
            pltpu.VMEM((count, 128, 256), bf16),
            pltpu.VMEM((count, 128, 256), f32),
            pltpu.VMEM((count, 16, 256), f32),
        ],
        compiler_params=pltpu.CompilerParams(vmem_limit_bytes=32 << 20),
        name="pair_and_one",
    )(*args)


def pack(total, gath, out_ref):
    out_ref[0:HALF, :] = total.astype(bf16)
    small = total[ONE + POOL :]
    out_ref[HALF:SENT, :] = (small - small.astype(bf16).astype(f32)).astype(bf16)
    at = SENT
    for piece in gath:
        out_ref[at : at + piece.shape[0], :] = piece
        at += piece.shape[0]


def first_kernel(keep_ref, came_ref, mean_ref, pos_ref, out_ref, col_ref):
    both = keep_ref[...] + came_ref[...]
    col = both[HALF:]
    col_ref[...] = col
    p1, p2, p3 = split3(pos_ref[:, 0, :])
    blank = jnp.zeros((2, 256), f32)
    border = jnp.concatenate(
        [
            jnp.concatenate([p1, p2], axis=1),
            jnp.concatenate([p3, jnp.zeros_like(p3)], axis=1),
            blank,
        ],
        axis=0,
    )
    gath = jnp.concatenate([mean_ref[...].astype(f32), col, border], axis=0).astype(bf16)
    pack(both[0:HALF], [gath], out_ref)


def first_call(keep, came, mean_rows, pos):
    count = mean_rows.shape[0]
    return pl.pallas_call(
        first_kernel,
        in_specs=[VMEM] * 4,
        out_specs=[VMEM] * 2,
        out_shape=[
            pltpu.VMEM((SENT + 2 * count + 8, 256), bf16),
            pltpu.VMEM((count, 256), f32),
        ],
        compiler_params=PARAMS,
        name="first_mix",
    )(near(keep), near(came), near(mean_rows), pos)


def add_up(own_ref, came_ref):
    total = own_ref[0:HALF, :].astype(f32) + came_ref[0:HALF, :].astype(f32)
    rest = own_ref[HALF:SENT, :].astype(f32) + came_ref[HALF:SENT, :].astype(f32)
    return jnp.concatenate([total[0 : ONE + POOL], total[ONE + POOL :] + rest], axis=0)


def mix_kernel(own_ref, came_ref, out_ref):
    pack(add_up(own_ref, came_ref), [own_ref[SENT:, :], came_ref[SENT:, :]], out_ref)


def mix_call(own, came):
    rows = SENT + 2 * (own.shape[0] - SENT)
    return pl.pallas_call(
        mix_kernel,
        in_specs=[VMEM] * 2,
        out_specs=VMEM,
        out_shape=pltpu.VMEM((rows, 256), bf16),
        compiler_params=PARAMS,
        name="mix",
    )(near(own), near(came))


def last_kernel(own_ref, came_ref, out_ref):
    out_ref[...] = add_up(own_ref, came_ref)


def last_call(own, came):
    return pl.pallas_call(
        last_kernel,
        in_specs=[VMEM] * 2,
        out_specs=VMEM,
        out_shape=pltpu.VMEM((HALF, 256), f32),
        compiler_params=PARAMS,
        name="last_mix",
    )(near(own), near(came))


def back_kernel(
    cot_ref, pre_ref, upd_ref, col_ref, pos_ref, ow_ref, mw_ref, dw_ref,
    grad_ref, link_ref, last_ref,
):
    count = col_ref.shape[0]
    back = dot(col_ref[...], mw_ref[...].astype(f32), 1, 1, HIGH) * (1.0 / 256)
    drifts = []
    for s in range(count):
        at = slice(s * 128, (s + 1) * 128)
        grad = cot_ref[at, :].astype(f32) + dot(pre_ref[at, :], ow_ref[...], 1, 1)
        grad_ref[at, :] = (grad + back[s : s + 1, :]).astype(bf16)
        drifts.append(dot(dw_ref[...], upd_ref[at, :], 1, 1))
    for s in range(count):
        here = [-pos_ref[c, s : s + 1, :] - step_tau * drifts[s][c : c + 1, :] for c in range(3)]
        if s < count - 1:
            jumps = [here[c] + pos_ref[c, s + 1 : s + 2, :] for c in range(3)]
            total = jumps[0] * jumps[0] + jumps[1] * jumps[1] + jumps[2] * jumps[2]
            link_ref[s : s + 1, :] = total * (1.0 / (12.0 * step_tau))
        else:
            link_ref[s : s + 1, :] = jnp.zeros((1, 128), f32)
            last_ref[...] = jnp.concatenate(here + [jnp.zeros((5, 128), f32)], axis=0)


def back_call(cot, pre, updated, col, pos, ow, mw, dw):
    args = (cot, near(pre), updated, near(col), pos, ow, mw, dw)
    return pl.pallas_call(
        back_kernel,
        in_specs=[VMEM] * len(args),
        out_specs=[VMEM] * 3,
        out_shape=[
            jax.ShapeDtypeStruct(cot.shape, bf16),
            pltpu.VMEM((col.shape[0], 128), f32),
            pltpu.VMEM((8, 128), f32),
        ],
        compiler_params=PARAMS,
        name="hidden_back",
    )(*args)


def mean_kernel(
    info_ref, own_ref, came_ref, link_ref, last_ref,
    mean_ref, out_link_ref,
    mean_all, col_all, border, *, scale, count,
):
    stride = 2 * count + 8
    half = (own_ref.shape[0] - SENT) // stride
    for d in range(2 * half):
        ref = own_ref if d < half else came_ref
        base = SENT + (d % half) * stride
        block = ref[base : base + stride, :].astype(f32)
        at = pl.ds(pl.multiple_of(info_ref[2 + d] * count, 8), count)
        mean_all[at, :] = block[0:count]
        col_all[at, :] = block[count : 2 * count]
        border[pl.ds(pl.multiple_of(info_ref[2 + d] * 8, 8), 8), :] = block[2 * count :]
    mean_ref[...] = scale * dot(mean_all[...].astype(bf16), col_all[...].astype(bf16), 0, 0)
    out_link_ref[...] = link_ref[...]
    pieces = border[pl.ds(pl.multiple_of(info_ref[0] * 8, 8), 8), :]
    point = pieces[0:3, 0:128] + pieces[0:3, 128:] + pieces[3:6, 0:128]
    jump = point + last_ref[0:3, :]
    total = jnp.sum(jump * jump, axis=0, keepdims=True) * (1.0 / (12.0 * step_tau))
    out_link_ref[count - 1 : count, :] = jnp.where(info_ref[1] == 1, 0.0, total)


def mean_call(info, own, came, link, last, scale, count):
    args = (info, near(own), near(came), near(link), near(last))
    devices = info.shape[0] - 2

    def body(*refs):
        mean_kernel(*refs, scale=scale, count=count)

    return pl.pallas_call(
        body,
        in_specs=[SMEM] + [VMEM] * 4,
        out_specs=[VMEM] * 2,
        out_shape=[
            jax.ShapeDtypeStruct((256, 256), f32),
            jax.ShapeDtypeStruct((count, 128), f32),
        ],
        scratch_shapes=[
            pltpu.VMEM((devices * count, 256), f32),
            pltpu.VMEM((devices * count, 256), f32),
            pltpu.VMEM((devices * 8, 256), f32),
        ],
        compiler_params=PARAMS,
        name="mean_and_link",
    )(*args)


def end_kernel(core_ref, own_ref, came_ref, one_ref, pool_ref, pair_ref, bias_ref, *, scale):
    def write(low_ref, high_ref):
        one_ref[0:ONE, :] = scale * low_ref[0:ONE, :]
        one_ref[ONE:, :] = scale * high_ref[0:ONE, :]
        pool_ref[0:POOL, :] = scale * low_ref[ONE : ONE + POOL, :]
        pool_ref[POOL:, :] = scale * high_ref[ONE : ONE + POOL, :]

        small = low_ref[ONE + POOL : HALF, :]
        rows = jnp.concatenate(
            [jnp.broadcast_to(small[r : r + 1], (8, 256)) for r in range(4)], axis=0
        )
        rows = jnp.where(iota((32, 256), 0) % 8 == iota((32, 256), 1) // 32, rows, 0.0)
        total = rows[:, 0:128] + rows[:, 128:]
        total = total + pltpu.roll(total, 64, 1)
        total = total + pltpu.roll(total, 32, 1)
        pair_ref[...] = (scale / 256.0) * total[:, 0:32].T
        bias_ref[...] = (scale / 256.0) * small[4:5, 0:32]

    core = core_ref[0]
    pl.when(core == 0)(lambda: write(own_ref, came_ref))
    pl.when(core == 1)(lambda: write(came_ref, own_ref))


def end_call(core, own, came, scale):
    def body(*refs):
        end_kernel(*refs, scale=scale)

    return pl.pallas_call(
        body,
        in_specs=[SMEM, VMEM, VMEM],
        out_specs=[VMEM] * 4,
        out_shape=[
            jax.ShapeDtypeStruct((256, 256), f32),
            jax.ShapeDtypeStruct((32, 256), f32),
            jax.ShapeDtypeStruct((32, 32), f32),
            jax.ShapeDtypeStruct((1, 32), f32),
        ],
        compiler_params=PARAMS,
        name="unpack",
    )(core, near(own), near(came))


def local(
    positions, hidden, cotangent, embed_weight, embed_bias, pair_weight, pair_bias,
    one_weight, pool_weight, mean_weight, one_bias, drift_weight,
):
    count, own_count, width = hidden.shape
    slices = lax.axis_size("slices")
    bits = slices.bit_length() - 1
    scale = 1.0 / math.sqrt(count * slices * own_count * lax.axis_size("ering"))
    core = lax.axis_index("ering").astype(jnp.int32)
    place = lax.axis_index("slices").astype(jnp.int32)

    def swap(array):
        return lax.ppermute(array, "ering", [(0, 1), (1, 0)])

    orders = [[(t + e) % bits for t in range(bits)] for e in range(2)]
    masks = [
        [sum(((d >> t) & 1) << orders[e][t] for t in range(bits)) for d in range(slices)]
        for e in range(2)
    ]
    owners = place ^ jnp.where(core == 0, jnp.array(masks[0]), jnp.array(masks[1]))
    info = jnp.concatenate(
        [
            jnp.minimum(place + 1, slices - 1).reshape(1),
            (place == slices - 1).astype(jnp.int32).reshape(1),
            owners.astype(jnp.int32),
        ]
    )
    core = core.reshape(1)

    other_pos = swap(positions)
    part_sum = jnp.sum(hidden.astype(f32), axis=1)
    other_sum = swap(part_sum)
    updated, pre, keep, send, mean_rows = main_call(
        core, positions, other_pos, embed_weight, embed_bias, pair_weight, pair_bias, hidden,
        cotangent, part_sum, other_sum, one_weight, pool_weight, mean_weight, one_bias,
    )
    state, col_total = first_call(keep, swap(send), mean_rows, positions)
    hidden_grad, link, last = back_call(
        cotangent.reshape(pre.shape), pre, updated, col_total, positions, one_weight,
        mean_weight, drift_weight,
    )
    for t in range(bits):
        pairs = [
            (s * 2 + e, (s ^ (1 << orders[e][t])) * 2 + e) for s in range(slices) for e in range(2)
        ]
        came = lax.ppermute(state, ("slices", "ering"), pairs)
        if t == bits - 1:
            came, hidden_grad, link, last = lax.optimization_barrier((came, hidden_grad, link, last))
        if t < bits - 1:
            state = mix_call(state, came)
    total = last_call(state, came)
    other_total = swap(total)
    mean_grad, link_terms = mean_call(info, state, came, link, last, scale, count)
    one_grad, pool_grad, pair_grad, bias_grad = end_call(core, total, other_total, scale)
    return (
        updated.reshape(hidden.shape),
        hidden_grad.reshape(hidden.shape),
        link_terms,
        pair_grad,
        bias_grad.reshape(-1),
        one_grad,
        pool_grad,
        mean_grad,
    )


def solution(mesh):
    in_specs = (
        P(None, ("groups", "slices"), "ering"),
        P(("groups", "slices"), "ering", None),
        P(("groups", "slices"), "ering", None),
    ) + (P(),) * 9
    out_specs = (
        P(("groups", "slices"), "ering", None),
        P(("groups", "slices"), "ering", None),
        P(("groups", "slices"), "ering"),
        P("groups", None),
        P("groups"),
        P("groups", None),
        P("groups", None),
        P("groups", None),
    )
    return jax.shard_map(local, mesh=mesh, in_specs=in_specs, out_specs=out_specs, check_vma=False)
```

```python
import math

import jax
import jax.numpy as jnp
from jax import lax
from jax.experimental import pallas as pl
from jax.experimental.pallas import tpu as pltpu
from jax.sharding import PartitionSpec as P

HIGH = lax.Precision.HIGHEST
f32 = jnp.float32
bf16 = jnp.bfloat16
step_tau = 0.5
ONE, POOL, SMALL = 128, 16, 8
HALF = ONE + POOL + SMALL
SENT = HALF + SMALL
COPIED = 5
PARAMS = pltpu.CompilerParams(vmem_limit_bytes=16 << 20)
VMEM = pl.BlockSpec(memory_space=pltpu.VMEM)
SMEM = pl.BlockSpec(memory_space=pltpu.SMEM)


def near(array):
    return pltpu.with_memory_space_constraint(array, pltpu.VMEM)


def far(array):
    return pltpu.with_memory_space_constraint(array, pltpu.HBM)


def dot(a, b, ca, cb, precision=None):
    return lax.dot_general(
        a, b, (((ca,), (cb,)), ((), ())), preferred_element_type=f32, precision=precision
    )


def split3(x):
    first = x.astype(bf16).astype(f32)
    rest = x - first
    second = rest.astype(bf16).astype(f32)
    return first, second, rest - second


def iota(shape, dim):
    return lax.broadcasted_iota(jnp.int32, shape, dim)


def pair_kernel(
    own_ref, other_ref, ew_ref, eb_ref, pw_ref, pb_ref, *refs
):
    pooled_ref, h_ref, g_ref, pre_ref = refs[COPIED : COPIED + 4]
    near_refs = refs[COPIED + 4 : 2 * COPIED + 4]
    copies = [
        pltpu.make_async_copy(refs[n], near_refs[n], refs[-1].at[n]) for n in range(COPIED)
    ]
    for copy in copies:
        copy.start()

    def ready():
        for copy in copies:
            copy.wait()

    def weigh(step):
        at = pl.ds(2 * step, 2)
        rows = near_refs[0][at].reshape(256, 256)
        pre_ref[at] = dot(rows, near_refs[2][...], 1, 0).reshape(2, 128, 256)

    pair_steps(
        own_ref, other_ref, ew_ref, eb_ref, pw_ref, pb_ref, pooled_ref, h_ref, g_ref,
        ready, weigh, *refs[2 * COPIED + 4 : -1],
    )


def pair_steps(
    own_ref, other_ref, ew_ref, eb_ref, pw_ref, pb_ref,
    pooled_ref, h_ref, g_ref, ready, weigh,
    embed_mat, block_mat, a_rows, feat_a, feat_b, bias_row, columns, misc_all,
    pre_a, pre_b, act_a, act_b, in_a, in_b, in_c, in_d, slope_a, slope_b, sum_a, sum_b, sum_c, sum_d,
):
    count = own_ref.shape[1]
    feats = (feat_a, feat_b)
    pre, acts, slopes = (pre_a, pre_b), (act_a, act_b), (slope_a, slope_b)
    ins, sums = (in_a, in_b, in_c, in_d), (sum_a, sum_b, sum_c, sum_d)

    def features(feat, at, first, size):
        lane = iota((size, 128), 1)
        square = jnp.ones((size, 128), f32)
        for c in range(3):
            spread = jnp.broadcast_to(
                columns[at, first : first + size, c : c + 1], (size, 128)
            )
            offset = spread - own_ref[c, pl.ds(at, 1), :]
            square = square + offset * offset
        radial = square * lax.rsqrt(square)
        misc = misc_all[at, first : first + size, :]
        high = radial.astype(bf16).astype(f32)
        low = radial - high
        high_turned = pltpu.roll(high, 64, 1)
        low_turned = pltpu.roll(low, 64, 1)
        left = lane < 64
        rows = slice(first, first + size)
        feat[0, rows, :128] = jnp.where(left, high, low_turned).astype(bf16)
        feat[0, rows, 128:] = jnp.where(left, high, misc).astype(bf16)
        feat[1, rows, :128] = jnp.where(left, high_turned, low).astype(bf16)
        feat[1, rows, 128:] = jnp.where(left, high_turned, misc).astype(bf16)

    wide = jnp.concatenate([ew_ref[...]] * 8, axis=1)
    w1, w2, w3 = split3(wide)
    row = iota((64, 256), 0)
    lane = iota((64, 256), 1)
    pieces = (w1, w2, w3, w1, w2, w1)
    misc = jnp.zeros((64, 256), f32)
    for c in range(3):
        for p in range(6):
            misc = jnp.where(row == 6 * c + p, -pieces[p][c : c + 1, :], misc)
    misc = misc.astype(bf16)
    for g in range(8):
        hit = row == g * 8 + lane // 32
        first = jnp.where(hit, w1[3:4, :], 0.0).astype(bf16)
        embed_mat[0:64, g * 256 : (g + 1) * 256] = first
        embed_mat[64:128, g * 256 : (g + 1) * 256] = first
        embed_mat[128:192, g * 256 : (g + 1) * 256] = jnp.where(hit, w2[3:4, :], 0.0).astype(bf16)
        embed_mat[192:256, g * 256 : (g + 1) * 256] = misc
    row = iota((256, 256), 0)
    lane = iota((256, 256), 1)
    tiled = jnp.concatenate([pw_ref[...].astype(f32).T] * 8, axis=1)
    tiled = jnp.concatenate([tiled] * 8, axis=0)
    block_mat[...] = jnp.where(row // 32 == lane // 32, tiled, 0.0).astype(bf16)
    bias_row[...] = jnp.broadcast_to(jnp.concatenate([pb_ref[...]] * 8, axis=1), (8, 256))
    wide_bias = jnp.concatenate([eb_ref[...]] * 8, axis=1)
    electron = iota((128, 256), 0)
    lane128 = iota((128, 256), 1)
    points = jnp.concatenate(
        [piece for c in range(3) for piece in split3(own_ref[c])], axis=0
    ).astype(bf16)
    for g in range(16):
        pick = jnp.where(electron == g * 8 + lane128 // 32, 1.0, 0.0).astype(bf16)
        spread = dot(points, pick, 1, 0)
        total = jnp.broadcast_to(wide_bias, (count, 256))
        for c in range(3):
            base = 3 * c * count
            point = (
                spread[base : base + count]
                + spread[base + count : base + 2 * count]
                + spread[base + 2 * count : base + 3 * count]
            )
            total = total + point * wide[c : c + 1, :]
        a_rows[:, g * 256 : (g + 1) * 256] = total
    blank = jnp.zeros((5, 256), f32)
    for at in range(count):
        stacked = jnp.concatenate(
            [
                jnp.concatenate(
                    [own_ref[c, at : at + 1, :], other_ref[c, at : at + 1, :]], axis=1
                )
                for c in range(3)
            ]
            + [blank],
            axis=0,
        )
        columns[at] = stacked.T
        spread = jnp.zeros((24, 256), f32)
        row = iota((24, 256), 0)
        for c in range(3):
            s1, s2, s3 = split3(stacked[c : c + 1, :])
            for p, piece in enumerate((s1, s1, s1, s2, s2, s3)):
                spread = jnp.where(row == 6 * c + p, piece, spread)
        zeros = jnp.zeros((64, 256), f32)
        misc_all[at] = jnp.concatenate([zeros, spread, zeros[0:40]], axis=0).T
    features(feat_a, 0, 0, 256)
    diagonal = iota((8, 256), 0) == iota((8, 256), 1) // 32
    block = iota((32, 256), 1) // 32

    def turn(step, places, started):
        def embed(n):
            at = 2 * step + n // 16
            half, inner = n % 16 // 8, n % 8
            out = dot(feats[n // 16][half], embed_mat[:, inner * 256 : (inner + 1) * 256], 1, 0)
            pre[n % 2][...] = out + a_rows[pl.ds(at, 1), n % 16 * 256 : (n % 16 + 1) * 256]

        def first_tanh(n):
            out = jnp.tanh(pre[n % 2][...])
            ins[n % 4][...] = out.astype(bf16)
            sums[n % 4][...] = jnp.sum(out.reshape(32, 8, 256), axis=0)

        def layer(n):
            acts[n % 2][...] = dot(ins[n % 4][...], block_mat[...], 1, 0) + bias_row[0:1, :]

        def slice_of(n):
            return jnp.maximum(2 * step - 1, 0) if n < 0 else 2 * step + n // 16

        def second_tanh(n):
            at, g = slice_of(n), n % 16
            act = jnp.tanh(acts[n % 2][...])
            total = sums[n % 4][...] + jnp.sum(act.reshape(32, 8, 256), axis=0)
            mean = jnp.sum(total, axis=0, keepdims=True) * (1.0 / 256)
            slope = 1.0 - act * act
            h_ref[at, g : g + 1, :] = jnp.sum(slope, axis=0, keepdims=True)
            pooled_ref[at, g * 8 : (g + 1) * 8, :] = jnp.where(diagonal, mean, 0.0)
            slopes[n % 2][...] = slope.astype(bf16)

        def outer(n):
            at, g = slice_of(n), n % 16
            product = dot(ins[n % 4][...], slopes[n % 2][...], 0, 0)
            picked = product[0:32]
            for q in range(1, 8):
                picked = jnp.where(block == q, product[q * 32 : (q + 1) * 32], picked)
            g_ref[at, g * 32 : (g + 1) * 32, :] = picked

        for place in places:
            for lag, stage in enumerate((embed, first_tanh, layer, second_tanh, outer)):
                if place - lag < started:
                    stage(place - lag)
            if started and place % 16 == 0:
                upcoming = jnp.minimum(2 * step + place // 16 + 1, count - 1)
                features(feats[1 - place // 16], upcoming, 0, 256)

    turns = count // 2

    def body(step, carry):
        weigh(step)
        turn(step, range(32), 32)
        return carry

    ready()
    lax.fori_loop(0, turns, body, 0)
    turn(turns, range(4), 0)


def pair_call(own, other, ew, eb, pw, pb, later):
    count = own.shape[1]
    args = (
        far(own), near(other), far(ew.T), far(eb.reshape(1, 32)), far(pw), far(pb.reshape(1, 32)),
    ) + tuple(far(a) for a in later)
    return pl.pallas_call(
        pair_kernel,
        in_specs=[VMEM] * 6 + [pl.BlockSpec(memory_space=pltpu.HBM)] * COPIED,
        out_specs=[VMEM] * (4 + COPIED),
        out_shape=[
            pltpu.VMEM((count, 128, 256), f32),
            pltpu.VMEM((count, 16, 256), f32),
            pltpu.VMEM((count, 512, 256), f32),
            pltpu.VMEM((count, 128, 256), f32),
        ]
        + [pltpu.VMEM(a.shape, a.dtype) for a in later],
        scratch_shapes=[
            pltpu.VMEM((256, 2048), bf16),
            pltpu.VMEM((256, 256), bf16),
            pltpu.VMEM((count, 4096), f32),
            pltpu.VMEM((2, 256, 256), bf16),
            pltpu.VMEM((2, 256, 256), bf16),
            pltpu.VMEM((8, 256), f32),
            pltpu.VMEM((count, 256, 8), f32),
            pltpu.VMEM((count, 256, 128), f32),
        ]
        + [pltpu.VMEM((256, 256), f32)] * 4
        + [pltpu.VMEM((256, 256), bf16)] * 6
        + [pltpu.VMEM((8, 256), f32)] * 4
        + [pltpu.SemaphoreType.DMA((COPIED,))],
        compiler_params=pltpu.CompilerParams(vmem_limit_bytes=24 << 20),
        name="pair_stage",
    )(*args)


def one_kernel(
    core_ref, hid_ref, cot_ref, one_pre_ref, pooled_ref, h_ref, g_ref, sum_a_ref, sum_b_ref,
    qw_ref, mw_ref, ob_ref,
    updated_ref, grad_ref, keep_ref, send_ref, mean_ref,
    back_all,
):
    count = sum_a_ref.shape[0]
    pool_mat = jnp.concatenate([qw_ref[...]] * 8, axis=0)
    mean_rows = ((sum_a_ref[...] + sum_b_ref[...]) * (1.0 / 256)).astype(bf16)
    mean_ref[...] = mean_rows
    per_slice = dot(mean_rows, mw_ref[...], 1, 0) + ob_ref[...]
    own_lanes = iota((256, 256), 0) % 8 == iota((256, 256), 1) // 32
    one_total = jnp.zeros((256, 256), f32)
    pool_total = jnp.zeros((256, 256), f32)
    pair_total = jnp.zeros((32, 256), f32)
    bias_total = jnp.zeros((32, 256), f32)
    parts = []

    def two(ref, n):
        value = ref[2 * n : 2 * n + 2]
        return value.reshape(2 * value.shape[1], 256)

    for step in range(count // 2 + 2):
        if step < count // 2:
            rows = slice(step * 256, (step + 1) * 256)
            shift = jnp.concatenate(
                [
                    jnp.broadcast_to(per_slice[n : n + 1, :], (128, 256))
                    for n in (2 * step, 2 * step + 1)
                ],
                axis=0,
            )
            pooled = two(pooled_ref, step).astype(bf16)
            act = jnp.tanh(two(one_pre_ref, step) + dot(pooled, pool_mat, 1, 0) + shift)
            updated_ref[rows, :] = (act + two(hid_ref, step).astype(f32)).astype(bf16)
            grad = (two(cot_ref, step).astype(f32) * (1.0 - act * act)).astype(bf16)
            grad_ref[rows, :] = grad
            wide = grad.astype(f32)
            parts.append(jnp.sum(wide[0:128], axis=0, keepdims=True))
            parts.append(jnp.sum(wide[128:], axis=0, keepdims=True))
        n = step - 1
        if 0 <= n < count // 2:
            grad = grad_ref[n * 256 : (n + 1) * 256, :]
            back = jnp.where(own_lanes, dot(grad, pool_mat, 1, 1), 0.0)
            back_all[n] = jnp.sum(back.reshape(32, 8, 256), axis=1)
            one_total = one_total + dot(two(hid_ref, n), grad, 0, 0)
            pool_total = pool_total + dot(two(pooled_ref, n).astype(bf16), grad, 0, 0)
        n = step - 2
        if 0 <= n < count // 2:
            bias_total = bias_total + back_all[n] * two(h_ref, n)
            for g in range(32):
                part = g_ref[2 * n + g // 16, g % 16 * 32 : (g % 16 + 1) * 32, :]
                pair_total = pair_total + part * back_all[n, g : g + 1, :]
    fold = jnp.where(iota((256, 256), 0) % 32 == iota((256, 256), 1) % 32, 1.0, 0.0)
    pool = pool_total[0:32]
    for q in range(1, 8):
        pool = pool + pool_total[q * 32 : (q + 1) * 32]
    bias_one = jnp.broadcast_to(jnp.sum(bias_total, axis=0, keepdims=True), (8, 256))
    folded = dot(jnp.concatenate([pair_total, bias_one], axis=0), fold, 1, 0, HIGH)
    picked = jnp.where(iota((32, 256), 0) % 8 == iota((32, 256), 1) // 32, folded[0:32], 0.0)
    packed = jnp.sum(picked.reshape(4, 8, 256), axis=1)
    small = jnp.concatenate([packed, folded[32:36]], axis=0)
    core = core_ref[0]

    @pl.when(core == 0)
    def _():
        keep_ref[0:ONE, :] = one_total[0:ONE]
        send_ref[0:ONE, :] = one_total[ONE:]
        keep_ref[ONE : ONE + POOL, :] = pool[0:POOL]
        send_ref[ONE : ONE + POOL, :] = pool[POOL:]

    @pl.when(core == 1)
    def _():
        send_ref[0:ONE, :] = one_total[0:ONE]
        keep_ref[0:ONE, :] = one_total[ONE:]
        send_ref[ONE : ONE + POOL, :] = pool[0:POOL]
        keep_ref[ONE : ONE + POOL, :] = pool[POOL:]

    keep_ref[ONE + POOL : HALF, :] = small
    send_ref[ONE + POOL : HALF, :] = small
    sums = jnp.concatenate(parts, axis=0)
    keep_ref[HALF:, :] = sums
    send_ref[HALF:, :] = sums


def one_call(core, hid, cot, one_pre, pooled, h_sums, g_sums, sum_a, sum_b, qw, mw, ob):
    count, rows, width = hid.shape
    args = (
        core, near(hid), near(cot), near(one_pre), near(pooled), near(h_sums), near(g_sums), near(sum_a),
        near(sum_b), near(qw), near(mw), far(ob.reshape(1, width)),
    )
    return pl.pallas_call(
        one_kernel,
        in_specs=[SMEM] + [VMEM] * 11,
        out_specs=[VMEM] * 5,
        out_shape=[
            jax.ShapeDtypeStruct((count * rows, width), bf16),
            pltpu.VMEM((count * rows, width), bf16),
            pltpu.VMEM((HALF + count, width), f32),
            pltpu.VMEM((HALF + count, width), f32),
            pltpu.VMEM((count, width), bf16),
        ],
        scratch_shapes=[pltpu.VMEM((count // 2, 32, 256), f32)],
        compiler_params=PARAMS,
        name="one_stage",
    )(*args)


def pack(total, gath, out_ref):
    out_ref[0:HALF, :] = total.astype(bf16)
    small = total[ONE + POOL :]
    out_ref[HALF:SENT, :] = (small - small.astype(bf16).astype(f32)).astype(bf16)
    at = SENT
    for piece in gath:
        out_ref[at : at + piece.shape[0], :] = piece
        at += piece.shape[0]


def first_kernel(keep_ref, came_ref, mean_ref, pos_ref, out_ref, col_ref):
    both = keep_ref[...] + came_ref[...]
    col = both[HALF:]
    col_ref[...] = col
    p1, p2, p3 = split3(pos_ref[:, 0, :])
    blank = jnp.zeros((2, 256), f32)
    border = jnp.concatenate(
        [
            jnp.concatenate([p1, p2], axis=1),
            jnp.concatenate([p3, jnp.zeros_like(p3)], axis=1),
            blank,
        ],
        axis=0,
    )
    gath = jnp.concatenate([mean_ref[...].astype(f32), col, border], axis=0).astype(bf16)
    pack(both[0:HALF], [gath], out_ref)


def first_call(keep, came, mean_rows, pos):
    count = mean_rows.shape[0]
    return pl.pallas_call(
        first_kernel,
        in_specs=[VMEM] * 4,
        out_specs=[VMEM] * 2,
        out_shape=[
            pltpu.VMEM((SENT + 2 * count + 8, 256), bf16),
            pltpu.VMEM((count, 256), f32),
        ],
        compiler_params=PARAMS,
        name="first_mix",
    )(near(keep), near(came), near(mean_rows), pos)


def add_up(own_ref, came_ref):
    total = own_ref[0:HALF, :].astype(f32) + came_ref[0:HALF, :].astype(f32)
    rest = own_ref[HALF:SENT, :].astype(f32) + came_ref[HALF:SENT, :].astype(f32)
    return jnp.concatenate([total[0 : ONE + POOL], total[ONE + POOL :] + rest], axis=0)


def mix_kernel(own_ref, came_ref, out_ref):
    pack(add_up(own_ref, came_ref), [own_ref[SENT:, :], came_ref[SENT:, :]], out_ref)


def mix_call(own, came):
    rows = SENT + 2 * (own.shape[0] - SENT)
    return pl.pallas_call(
        mix_kernel,
        in_specs=[VMEM] * 2,
        out_specs=VMEM,
        out_shape=pltpu.VMEM((rows, 256), bf16),
        compiler_params=PARAMS,
        name="mix",
    )(near(own), near(came))


def last_kernel(own_ref, came_ref, out_ref):
    out_ref[...] = add_up(own_ref, came_ref)


def last_call(own, came):
    return pl.pallas_call(
        last_kernel,
        in_specs=[VMEM] * 2,
        out_specs=VMEM,
        out_shape=pltpu.VMEM((HALF, 256), f32),
        compiler_params=PARAMS,
        name="last_mix",
    )(near(own), near(came))


def back_kernel(
    cot_ref, pre_ref, upd_ref, col_ref, pos_ref, ow_ref, mw_ref, dw_ref,
    grad_ref, link_ref, last_ref,
):
    count = col_ref.shape[0]
    back = dot(col_ref[...], mw_ref[...].astype(f32), 1, 1, HIGH) * (1.0 / 256)
    drifts = []
    for s in range(count):
        at = slice(s * 128, (s + 1) * 128)
        grad = cot_ref[at, :].astype(f32) + dot(pre_ref[at, :], ow_ref[...], 1, 1)
        grad_ref[at, :] = (grad + back[s : s + 1, :]).astype(bf16)
        drifts.append(dot(dw_ref[...], upd_ref[at, :], 1, 1))
    for s in range(count):
        here = [-pos_ref[c, s : s + 1, :] - step_tau * drifts[s][c : c + 1, :] for c in range(3)]
        if s < count - 1:
            jumps = [here[c] + pos_ref[c, s + 1 : s + 2, :] for c in range(3)]
            total = jumps[0] * jumps[0] + jumps[1] * jumps[1] + jumps[2] * jumps[2]
            link_ref[s : s + 1, :] = total * (1.0 / (12.0 * step_tau))
        else:
            link_ref[s : s + 1, :] = jnp.zeros((1, 128), f32)
            last_ref[...] = jnp.concatenate(here + [jnp.zeros((5, 128), f32)], axis=0)


def back_call(cot, pre, updated, col, pos, ow, mw, dw):
    args = (near(cot), near(pre), far(updated), near(col), far(pos), near(ow), near(mw), far(dw))
    return pl.pallas_call(
        back_kernel,
        in_specs=[VMEM] * len(args),
        out_specs=[VMEM] * 3,
        out_shape=[
            jax.ShapeDtypeStruct(cot.shape, bf16),
            pltpu.VMEM((col.shape[0], 128), f32),
            pltpu.VMEM((8, 128), f32),
        ],
        compiler_params=PARAMS,
        name="hidden_back",
    )(*args)


def mean_kernel(
    info_ref, own_ref, came_ref, link_ref, last_ref,
    mean_ref, out_link_ref,
    mean_all, col_all, border, *, scale, count, masks,
):
    stride = 2 * count + 8
    half = (own_ref.shape[0] - SENT) // stride
    place, core = info_ref[0], info_ref[1]
    for d in range(2 * half):
        owner = place ^ jnp.where(core == 0, masks[0][d], masks[1][d])
        ref = own_ref if d < half else came_ref
        base = SENT + (d % half) * stride
        block = ref[base : base + stride, :].astype(f32)
        at = pl.ds(pl.multiple_of(owner * count, 8), count)
        mean_all[at, :] = block[0:count]
        col_all[at, :] = block[count : 2 * count]
        border[pl.ds(pl.multiple_of(owner * 8, 8), 8), :] = block[2 * count :]
    mean_ref[...] = scale * dot(mean_all[...].astype(bf16), col_all[...].astype(bf16), 0, 0)
    out_link_ref[...] = link_ref[...]
    pieces = border[pl.ds(pl.multiple_of(jnp.minimum(place + 1, 2 * half - 1) * 8, 8), 8), :]
    point = pieces[0:3, 0:128] + pieces[0:3, 128:] + pieces[3:6, 0:128]
    jump = point + last_ref[0:3, :]
    total = jnp.sum(jump * jump, axis=0, keepdims=True) * (1.0 / (12.0 * step_tau))
    out_link_ref[count - 1 : count, :] = jnp.where(place == 2 * half - 1, 0.0, total)


def mean_call(info, own, came, link, last, scale, count, masks):
    args = (info, near(own), near(came), near(link), near(last))
    devices = len(masks[0])

    def body(*refs):
        mean_kernel(*refs, scale=scale, count=count, masks=masks)

    return pl.pallas_call(
        body,
        in_specs=[SMEM] + [VMEM] * 4,
        out_specs=[VMEM] * 2,
        out_shape=[
            jax.ShapeDtypeStruct((256, 256), f32),
            jax.ShapeDtypeStruct((count, 128), f32),
        ],
        scratch_shapes=[
            pltpu.VMEM((devices * count, 256), f32),
            pltpu.VMEM((devices * count, 256), f32),
            pltpu.VMEM((devices * 8, 256), f32),
        ],
        compiler_params=PARAMS,
        name="mean_and_link",
    )(*args)


def end_kernel(core_ref, own_ref, came_ref, one_ref, pool_ref, pair_ref, bias_ref, *, scale):
    def write(low_ref, high_ref):
        one_ref[0:ONE, :] = scale * low_ref[0:ONE, :]
        one_ref[ONE:, :] = scale * high_ref[0:ONE, :]
        pool_ref[0:POOL, :] = scale * low_ref[ONE : ONE + POOL, :]
        pool_ref[POOL:, :] = scale * high_ref[ONE : ONE + POOL, :]

        small = low_ref[ONE + POOL : HALF, :]
        rows = jnp.concatenate(
            [jnp.broadcast_to(small[r : r + 1], (8, 256)) for r in range(4)], axis=0
        )
        rows = jnp.where(iota((32, 256), 0) % 8 == iota((32, 256), 1) // 32, rows, 0.0)
        total = rows[:, 0:128] + rows[:, 128:]
        total = total + pltpu.roll(total, 64, 1)
        total = total + pltpu.roll(total, 32, 1)
        pair_ref[...] = (scale / 256.0) * total[:, 0:32].T
        bias_ref[...] = (scale / 256.0) * small[4:5, 0:32]

    core = core_ref[0]
    pl.when(core == 0)(lambda: write(own_ref, came_ref))
    pl.when(core == 1)(lambda: write(came_ref, own_ref))


def end_call(core, own, came, scale):
    def body(*refs):
        end_kernel(*refs, scale=scale)

    return pl.pallas_call(
        body,
        in_specs=[SMEM, VMEM, VMEM],
        out_specs=[VMEM] * 4,
        out_shape=[
            jax.ShapeDtypeStruct((256, 256), f32),
            jax.ShapeDtypeStruct((32, 256), f32),
            jax.ShapeDtypeStruct((32, 32), f32),
            jax.ShapeDtypeStruct((1, 32), f32),
        ],
        compiler_params=PARAMS,
        name="unpack",
    )(core, near(own), near(came))


def local(
    positions, hidden, cotangent, embed_weight, embed_bias, pair_weight, pair_bias,
    one_weight, pool_weight, mean_weight, one_bias, drift_weight,
):
    count, own_count, width = hidden.shape
    slices = lax.axis_size("slices")
    bits = slices.bit_length() - 1
    scale = 1.0 / math.sqrt(count * slices * own_count * lax.axis_size("ering"))
    core = lax.axis_index("ering").astype(jnp.int32)
    place = lax.axis_index("slices").astype(jnp.int32)

    def swap(array):
        return lax.ppermute(array, "ering", [(0, 1), (1, 0)])

    orders = [[(t + e) % bits for t in range(bits)] for e in range(2)]
    masks = [
        [sum(((d >> t) & 1) << orders[e][t] for t in range(bits)) for d in range(slices)]
        for e in range(2)
    ]
    info = jnp.stack([place, core])
    core = core.reshape(1)

    other_pos = swap(positions)
    part_sum = jnp.sum(hidden.astype(f32), axis=1)
    other_sum = swap(part_sum)
    pooled, h_sums, g_sums, one_pre, hid_near, cot_near, one_near, pool_near, mean_near = pair_call(
        positions, other_pos, embed_weight, embed_bias, pair_weight, pair_bias,
        (hidden, cotangent, one_weight, pool_weight, mean_weight),
    )
    updated, pre, keep, send, mean_rows = one_call(
        core, hid_near, cot_near, one_pre, pooled, h_sums, g_sums, part_sum, other_sum,
        pool_near, mean_near, one_bias,
    )
    state, col_total = first_call(keep, swap(send), mean_rows, positions)
    hidden_grad, link, last = back_call(
        cot_near.reshape(pre.shape), pre, updated, col_total, positions, one_near,
        mean_near, drift_weight,
    )
    for t in range(bits):
        pairs = [
            (s * 2 + e, (s ^ (1 << orders[e][t])) * 2 + e) for s in range(slices) for e in range(2)
        ]
        came = lax.ppermute(state, ("slices", "ering"), pairs)
        if t == bits - 1:
            came, hidden_grad, link, last = lax.optimization_barrier((came, hidden_grad, link, last))
        if t < bits - 1:
            state = mix_call(state, came)
    total = last_call(state, came)
    other_total = swap(total)
    mean_grad, link_terms = mean_call(info, state, came, link, last, scale, count, masks)
    one_grad, pool_grad, pair_grad, bias_grad = end_call(core, total, other_total, scale)
    return (
        updated.reshape(hidden.shape),
        hidden_grad.reshape(hidden.shape),
        link_terms,
        pair_grad,
        bias_grad.reshape(-1),
        one_grad,
        pool_grad,
        mean_grad,
    )


def solution(mesh):
    in_specs = (
        P(None, ("groups", "slices"), "ering"),
        P(("groups", "slices"), "ering", None),
        P(("groups", "slices"), "ering", None),
    ) + (P(),) * 9
    out_specs = (
        P(("groups", "slices"), "ering", None),
        P(("groups", "slices"), "ering", None),
        P(("groups", "slices"), "ering"),
        P("groups", None),
        P("groups"),
        P("groups", None),
        P("groups", None),
        P("groups", None),
    )
    return jax.shard_map(local, mesh=mesh, in_specs=in_specs, out_specs=out_specs, check_vma=False)
```

```python
import math

import jax
import jax.numpy as jnp
from jax import lax
from jax.experimental import pallas as pl
from jax.experimental.pallas import tpu as pltpu
from jax.sharding import PartitionSpec as P

HIGH = lax.Precision.HIGHEST
f32 = jnp.float32
bf16 = jnp.bfloat16
step_tau = 0.5
ONE, POOL, SMALL = 128, 16, 8
HALF = ONE + POOL + SMALL
SENT = HALF + SMALL
COPIED = 5
PARAMS = pltpu.CompilerParams(vmem_limit_bytes=16 << 20)
VMEM = pl.BlockSpec(memory_space=pltpu.VMEM)
SMEM = pl.BlockSpec(memory_space=pltpu.SMEM)


def near(array):
    return pltpu.with_memory_space_constraint(array, pltpu.VMEM)


def far(array):
    return pltpu.with_memory_space_constraint(array, pltpu.HBM)


def dot(a, b, ca, cb, precision=None):
    return lax.dot_general(
        a, b, (((ca,), (cb,)), ((), ())), preferred_element_type=f32, precision=precision
    )


def split3(x):
    first = x.astype(bf16).astype(f32)
    rest = x - first
    second = rest.astype(bf16).astype(f32)
    return first, second, rest - second


def iota(shape, dim):
    return lax.broadcasted_iota(jnp.int32, shape, dim)


def pair_kernel(
    own_ref, other_ref, ew_ref, eb_ref, pw_ref, pb_ref, *refs
):
    pooled_ref, h_ref, g_ref, pre_ref = refs[COPIED : COPIED + 4]
    near_refs = refs[COPIED + 4 : 2 * COPIED + 4]
    copies = [
        pltpu.make_async_copy(refs[n], near_refs[n], refs[-1].at[n]) for n in range(COPIED)
    ]
    for copy in copies:
        copy.start()

    def ready():
        for copy in copies:
            copy.wait()

    def weigh(step):
        at = pl.ds(2 * step, 2)
        rows = near_refs[0][at].reshape(256, 256)
        pre_ref[at] = dot(rows, near_refs[2][...], 1, 0).reshape(2, 128, 256)

    pair_steps(
        own_ref, other_ref, ew_ref, eb_ref, pw_ref, pb_ref, pooled_ref, h_ref, g_ref,
        ready, weigh, *refs[2 * COPIED + 4 : -1],
    )


def pair_steps(
    own_ref, other_ref, ew_ref, eb_ref, pw_ref, pb_ref,
    pooled_ref, h_ref, g_ref, ready, weigh,
    embed_mat, block_mat, a_rows, feat_a, feat_b, bias_row,
    pre_a, pre_b, act_a, act_b, in_a, in_b, in_c, in_d, slope_a, slope_b, sum_a, sum_b, sum_c, sum_d,
):
    count = own_ref.shape[1]
    feats = (feat_a, feat_b)
    pre, acts, slopes = (pre_a, pre_b), (act_a, act_b), (slope_a, slope_b)
    ins, sums = (in_a, in_b, in_c, in_d), (sum_a, sum_b, sum_c, sum_d)

    def features(feat, at):
        size = 256
        points = [
            jnp.concatenate([ref[c, pl.ds(at, 1), :] for ref in (own_ref, other_ref)], axis=1)
            for c in range(3)
        ]
        columns = jnp.concatenate(points + [jnp.zeros((5, 256), f32)], axis=0).T
        misc = jnp.zeros((24, 256), f32)
        row = iota((24, 256), 0)
        for c in range(3):
            s1, s2, s3 = split3(points[c])
            for p, piece in enumerate((s1, s1, s1, s2, s2, s3)):
                misc = jnp.where(row == 6 * c + p, piece, misc)
        zeros = jnp.zeros((64, 256), f32)
        misc = jnp.concatenate([zeros, misc, zeros[0:40]], axis=0).T
        lane = iota((size, 128), 1)
        square = jnp.ones((size, 128), f32)
        for c in range(3):
            spread = jnp.broadcast_to(columns[:, c : c + 1], (size, 128))
            offset = spread - own_ref[c, pl.ds(at, 1), :]
            square = square + offset * offset
        radial = square * lax.rsqrt(square)
        high = radial.astype(bf16).astype(f32)
        low = radial - high
        high_turned = pltpu.roll(high, 64, 1)
        low_turned = pltpu.roll(low, 64, 1)
        left = lane < 64
        feat[0, :, :128] = jnp.where(left, high, low_turned).astype(bf16)
        feat[0, :, 128:] = jnp.where(left, high, misc).astype(bf16)
        feat[1, :, :128] = jnp.where(left, high_turned, low).astype(bf16)
        feat[1, :, 128:] = jnp.where(left, high_turned, misc).astype(bf16)

    wide = jnp.concatenate([ew_ref[...]] * 8, axis=1)
    w1, w2, w3 = split3(wide)
    row = iota((64, 256), 0)
    lane = iota((64, 256), 1)
    pieces = (w1, w2, w3, w1, w2, w1)
    misc = jnp.zeros((64, 256), f32)
    for c in range(3):
        for p in range(6):
            misc = jnp.where(row == 6 * c + p, -pieces[p][c : c + 1, :], misc)
    misc = misc.astype(bf16)
    for g in range(8):
        hit = row == g * 8 + lane // 32
        first = jnp.where(hit, w1[3:4, :], 0.0).astype(bf16)
        embed_mat[0:64, g * 256 : (g + 1) * 256] = first
        embed_mat[64:128, g * 256 : (g + 1) * 256] = first
        embed_mat[128:192, g * 256 : (g + 1) * 256] = jnp.where(hit, w2[3:4, :], 0.0).astype(bf16)
        embed_mat[192:256, g * 256 : (g + 1) * 256] = misc
    row = iota((256, 256), 0)
    lane = iota((256, 256), 1)
    tiled = jnp.concatenate([pw_ref[...].astype(f32).T] * 8, axis=1)
    tiled = jnp.concatenate([tiled] * 8, axis=0)
    block_mat[...] = jnp.where(row // 32 == lane // 32, tiled, 0.0).astype(bf16)
    bias_row[...] = jnp.broadcast_to(jnp.concatenate([pb_ref[...]] * 8, axis=1), (8, 256))
    wide_bias = jnp.concatenate([eb_ref[...]] * 8, axis=1)
    electron = iota((128, 256), 0)
    lane128 = iota((128, 256), 1)
    points = jnp.concatenate(
        [piece for c in range(3) for piece in split3(own_ref[c])], axis=0
    ).astype(bf16)
    for g in range(16):
        pick = jnp.where(electron == g * 8 + lane128 // 32, 1.0, 0.0).astype(bf16)
        spread = dot(points, pick, 1, 0)
        total = jnp.broadcast_to(wide_bias, (count, 256))
        for c in range(3):
            base = 3 * c * count
            point = (
                spread[base : base + count]
                + spread[base + count : base + 2 * count]
                + spread[base + 2 * count : base + 3 * count]
            )
            total = total + point * wide[c : c + 1, :]
        a_rows[:, g * 256 : (g + 1) * 256] = total
    features(feat_a, 0)
    diagonal = iota((8, 256), 0) == iota((8, 256), 1) // 32
    block = iota((32, 256), 1) // 32

    def turn(step, places, started):
        def embed(n):
            at = 2 * step + n // 16
            half, inner = n % 16 // 8, n % 8
            out = dot(feats[n // 16][half], embed_mat[:, inner * 256 : (inner + 1) * 256], 1, 0)
            pre[n % 2][...] = out + a_rows[pl.ds(at, 1), n % 16 * 256 : (n % 16 + 1) * 256]

        def first_tanh(n):
            out = jnp.tanh(pre[n % 2][...])
            ins[n % 4][...] = out.astype(bf16)
            sums[n % 4][...] = jnp.sum(out.reshape(32, 8, 256), axis=0)

        def layer(n):
            acts[n % 2][...] = dot(ins[n % 4][...], block_mat[...], 1, 0) + bias_row[0:1, :]

        def slice_of(n):
            return jnp.maximum(2 * step - 1, 0) if n < 0 else 2 * step + n // 16

        def second_tanh(n):
            at, g = slice_of(n), n % 16
            act = jnp.tanh(acts[n % 2][...])
            total = sums[n % 4][...] + jnp.sum(act.reshape(32, 8, 256), axis=0)
            mean = jnp.sum(total, axis=0, keepdims=True) * (1.0 / 256)
            slope = 1.0 - act * act
            h_ref[at, g : g + 1, :] = jnp.sum(slope, axis=0, keepdims=True)
            pooled_ref[at, g * 8 : (g + 1) * 8, :] = jnp.where(diagonal, mean, 0.0)
            slopes[n % 2][...] = slope.astype(bf16)

        def outer(n):
            at, g = slice_of(n), n % 16
            product = dot(ins[n % 4][...], slopes[n % 2][...], 0, 0)
            picked = product[0:32]
            for q in range(1, 8):
                picked = jnp.where(block == q, product[q * 32 : (q + 1) * 32], picked)
            g_ref[at, g * 32 : (g + 1) * 32, :] = picked

        for place in places:
            for lag, stage in enumerate((embed, first_tanh, layer, second_tanh, outer)):
                if place - lag < started:
                    stage(place - lag)
            if started and place % 16 == 0:
                upcoming = jnp.minimum(2 * step + place // 16 + 1, count - 1)
                features(feats[1 - place // 16], upcoming)

    turns = count // 2

    def body(step, carry):
        pl.when(step == 1)(ready)
        pl.when(step >= 1)(lambda: weigh(step - 1))
        turn(step, range(32), 32)
        return carry

    lax.fori_loop(0, turns, body, 0)
    if turns == 1:
        ready()
    weigh(turns - 1)
    turn(turns, range(4), 0)


def pair_call(own, other, ew, eb, pw, pb, later):
    count = own.shape[1]
    args = (
        far(own), near(other), far(ew.T), far(eb.reshape(1, 32)), far(pw), far(pb.reshape(1, 32)),
    ) + tuple(far(a) for a in later)
    return pl.pallas_call(
        pair_kernel,
        in_specs=[VMEM] * 6 + [pl.BlockSpec(memory_space=pltpu.HBM)] * COPIED,
        out_specs=[VMEM] * (4 + COPIED),
        out_shape=[
            pltpu.VMEM((count, 128, 256), f32),
            pltpu.VMEM((count, 16, 256), f32),
            pltpu.VMEM((count, 512, 256), f32),
            pltpu.VMEM((count, 128, 256), f32),
        ]
        + [pltpu.VMEM(a.shape, a.dtype) for a in later],
        scratch_shapes=[
            pltpu.VMEM((256, 2048), bf16),
            pltpu.VMEM((256, 256), bf16),
            pltpu.VMEM((count, 4096), f32),
            pltpu.VMEM((2, 256, 256), bf16),
            pltpu.VMEM((2, 256, 256), bf16),
            pltpu.VMEM((8, 256), f32),
        ]
        + [pltpu.VMEM((256, 256), f32)] * 4
        + [pltpu.VMEM((256, 256), bf16)] * 6
        + [pltpu.VMEM((8, 256), f32)] * 4
        + [pltpu.SemaphoreType.DMA((COPIED,))],
        compiler_params=pltpu.CompilerParams(vmem_limit_bytes=24 << 20),
        name="pair_stage",
    )(*args)


def one_kernel(
    core_ref, hid_ref, cot_ref, one_pre_ref, pooled_ref, h_ref, g_ref, sum_a_ref, sum_b_ref,
    qw_ref, mw_ref, ob_ref,
    updated_ref, grad_ref, keep_ref, send_ref, mean_ref,
    back_all,
):
    count = sum_a_ref.shape[0]
    pool_mat = jnp.concatenate([qw_ref[...]] * 8, axis=0)
    mean_rows = ((sum_a_ref[...] + sum_b_ref[...]) * (1.0 / 256)).astype(bf16)
    mean_ref[...] = mean_rows
    per_slice = dot(mean_rows, mw_ref[...], 1, 0) + ob_ref[...]
    own_lanes = iota((256, 256), 0) % 8 == iota((256, 256), 1) // 32
    one_total = jnp.zeros((256, 256), f32)
    pool_total = jnp.zeros((256, 256), f32)
    pair_total = jnp.zeros((32, 256), f32)
    bias_total = jnp.zeros((32, 256), f32)
    parts = []

    def two(ref, n):
        value = ref[2 * n : 2 * n + 2]
        return value.reshape(2 * value.shape[1], 256)

    for step in range(count // 2 + 2):
        if step < count // 2:
            rows = slice(step * 256, (step + 1) * 256)
            shift = jnp.concatenate(
                [
                    jnp.broadcast_to(per_slice[n : n + 1, :], (128, 256))
                    for n in (2 * step, 2 * step + 1)
                ],
                axis=0,
            )
            pooled = two(pooled_ref, step).astype(bf16)
            act = jnp.tanh(two(one_pre_ref, step) + dot(pooled, pool_mat, 1, 0) + shift)
            updated_ref[rows, :] = (act + two(hid_ref, step).astype(f32)).astype(bf16)
            grad = (two(cot_ref, step).astype(f32) * (1.0 - act * act)).astype(bf16)
            grad_ref[rows, :] = grad
            wide = grad.astype(f32)
            parts.append(jnp.sum(wide[0:128], axis=0, keepdims=True))
            parts.append(jnp.sum(wide[128:], axis=0, keepdims=True))
        n = step - 1
        if 0 <= n < count // 2:
            grad = grad_ref[n * 256 : (n + 1) * 256, :]
            back = jnp.where(own_lanes, dot(grad, pool_mat, 1, 1), 0.0)
            back_all[n] = jnp.sum(back.reshape(32, 8, 256), axis=1)
            one_total = one_total + dot(two(hid_ref, n), grad, 0, 0)
            pool_total = pool_total + dot(two(pooled_ref, n).astype(bf16), grad, 0, 0)
        n = step - 2
        if 0 <= n < count // 2:
            bias_total = bias_total + back_all[n] * two(h_ref, n)
            for g in range(32):
                part = g_ref[2 * n + g // 16, g % 16 * 32 : (g % 16 + 1) * 32, :]
                pair_total = pair_total + part * back_all[n, g : g + 1, :]
    fold = jnp.where(iota((256, 256), 0) % 32 == iota((256, 256), 1) % 32, 1.0, 0.0)
    pool = pool_total[0:32]
    for q in range(1, 8):
        pool = pool + pool_total[q * 32 : (q + 1) * 32]
    bias_one = jnp.broadcast_to(jnp.sum(bias_total, axis=0, keepdims=True), (8, 256))
    folded = dot(jnp.concatenate([pair_total, bias_one], axis=0), fold, 1, 0, HIGH)
    picked = jnp.where(iota((32, 256), 0) % 8 == iota((32, 256), 1) // 32, folded[0:32], 0.0)
    packed = jnp.sum(picked.reshape(4, 8, 256), axis=1)
    small = jnp.concatenate([packed, folded[32:36]], axis=0)
    core = core_ref[0]

    @pl.when(core == 0)
    def _():
        keep_ref[0:ONE, :] = one_total[0:ONE]
        send_ref[0:ONE, :] = one_total[ONE:]
        keep_ref[ONE : ONE + POOL, :] = pool[0:POOL]
        send_ref[ONE : ONE + POOL, :] = pool[POOL:]

    @pl.when(core == 1)
    def _():
        send_ref[0:ONE, :] = one_total[0:ONE]
        keep_ref[0:ONE, :] = one_total[ONE:]
        send_ref[ONE : ONE + POOL, :] = pool[0:POOL]
        keep_ref[ONE : ONE + POOL, :] = pool[POOL:]

    keep_ref[ONE + POOL : HALF, :] = small
    send_ref[ONE + POOL : HALF, :] = small
    sums = jnp.concatenate(parts, axis=0)
    keep_ref[HALF:, :] = sums
    send_ref[HALF:, :] = sums


def one_call(core, hid, cot, one_pre, pooled, h_sums, g_sums, sum_a, sum_b, qw, mw, ob):
    count, rows, width = hid.shape
    args = (
        core, near(hid), near(cot), near(one_pre), near(pooled), near(h_sums), near(g_sums), near(sum_a),
        near(sum_b), near(qw), near(mw), far(ob.reshape(1, width)),
    )
    return pl.pallas_call(
        one_kernel,
        in_specs=[SMEM] + [VMEM] * 11,
        out_specs=[VMEM] * 5,
        out_shape=[
            pltpu.VMEM((count * rows, width), bf16),
            pltpu.VMEM((count * rows, width), bf16),
            pltpu.VMEM((HALF + count, width), f32),
            pltpu.VMEM((HALF + count, width), f32),
            pltpu.VMEM((count, width), bf16),
        ],
        scratch_shapes=[pltpu.VMEM((count // 2, 32, 256), f32)],
        compiler_params=PARAMS,
        name="one_stage",
    )(*args)


def pack(total, gath, out_ref):
    out_ref[0:HALF, :] = total.astype(bf16)
    small = total[ONE + POOL :]
    out_ref[HALF:SENT, :] = (small - small.astype(bf16).astype(f32)).astype(bf16)
    at = SENT
    for piece in gath:
        out_ref[at : at + piece.shape[0], :] = piece
        at += piece.shape[0]


def first_kernel(keep_ref, came_ref, mean_ref, pos_ref, out_ref, col_ref):
    both = keep_ref[...] + came_ref[...]
    col = both[HALF:]
    col_ref[...] = col
    p1, p2, p3 = split3(pos_ref[:, 0, :])
    blank = jnp.zeros((2, 256), f32)
    border = jnp.concatenate(
        [
            jnp.concatenate([p1, p2], axis=1),
            jnp.concatenate([p3, jnp.zeros_like(p3)], axis=1),
            blank,
        ],
        axis=0,
    )
    gath = jnp.concatenate([mean_ref[...].astype(f32), col, border], axis=0).astype(bf16)
    pack(both[0:HALF], [gath], out_ref)


def first_call(keep, came, mean_rows, pos):
    count = mean_rows.shape[0]
    return pl.pallas_call(
        first_kernel,
        in_specs=[VMEM] * 4,
        out_specs=[VMEM] * 2,
        out_shape=[
            pltpu.VMEM((SENT + 2 * count + 8, 256), bf16),
            pltpu.VMEM((count, 256), f32),
        ],
        compiler_params=PARAMS,
        name="first_mix",
    )(near(keep), near(came), near(mean_rows), pos)


def add_up(own_ref, came_ref):
    total = own_ref[0:HALF, :].astype(f32) + came_ref[0:HALF, :].astype(f32)
    rest = own_ref[HALF:SENT, :].astype(f32) + came_ref[HALF:SENT, :].astype(f32)
    return jnp.concatenate([total[0 : ONE + POOL], total[ONE + POOL :] + rest], axis=0)


def mix_kernel(own_ref, came_ref, out_ref):
    pack(add_up(own_ref, came_ref), [own_ref[SENT:, :], came_ref[SENT:, :]], out_ref)


def mix_call(own, came):
    rows = SENT + 2 * (own.shape[0] - SENT)
    return pl.pallas_call(
        mix_kernel,
        in_specs=[VMEM] * 2,
        out_specs=VMEM,
        out_shape=pltpu.VMEM((rows, 256), bf16),
        compiler_params=PARAMS,
        name="mix",
    )(near(own), near(came))


def last_kernel(own_ref, came_ref, out_ref):
    out_ref[...] = add_up(own_ref, came_ref)


def last_call(own, came):
    return pl.pallas_call(
        last_kernel,
        in_specs=[VMEM] * 2,
        out_specs=VMEM,
        out_shape=pltpu.VMEM((HALF, 256), f32),
        compiler_params=PARAMS,
        name="last_mix",
    )(near(own), near(came))


def back_kernel(
    cot_ref, pre_ref, upd_ref, col_ref, pos_ref, ow_ref, mw_ref, dw_ref,
    grad_ref, out_ref, link_ref, last_ref,
):
    count = col_ref.shape[0]
    back = dot(col_ref[...], mw_ref[...].astype(f32), 1, 1, HIGH) * (1.0 / 256)
    drifts = []
    for s in range(count):
        at = slice(s * 128, (s + 1) * 128)
        grad = cot_ref[at, :].astype(f32) + dot(pre_ref[at, :], ow_ref[...], 1, 1)
        grad_ref[at, :] = (grad + back[s : s + 1, :]).astype(bf16)
        drifts.append(dot(dw_ref[...], upd_ref[at, :], 1, 1))
        out_ref[at, :] = upd_ref[at, :]
    for s in range(count):
        here = [-pos_ref[c, s : s + 1, :] - step_tau * drifts[s][c : c + 1, :] for c in range(3)]
        if s < count - 1:
            jumps = [here[c] + pos_ref[c, s + 1 : s + 2, :] for c in range(3)]
            total = jumps[0] * jumps[0] + jumps[1] * jumps[1] + jumps[2] * jumps[2]
            link_ref[s : s + 1, :] = total * (1.0 / (12.0 * step_tau))
        else:
            link_ref[s : s + 1, :] = jnp.zeros((1, 128), f32)
            last_ref[...] = jnp.concatenate(here + [jnp.zeros((5, 128), f32)], axis=0)


def back_call(cot, pre, updated, col, pos, ow, mw, dw):
    args = (near(cot), near(pre), near(updated), near(col), far(pos), near(ow), near(mw), far(dw))
    return pl.pallas_call(
        back_kernel,
        in_specs=[VMEM] * len(args),
        out_specs=[VMEM] * 4,
        out_shape=[
            jax.ShapeDtypeStruct(cot.shape, bf16),
            jax.ShapeDtypeStruct(cot.shape, bf16),
            pltpu.VMEM((col.shape[0], 128), f32),
            pltpu.VMEM((8, 128), f32),
        ],
        compiler_params=PARAMS,
        name="hidden_back",
    )(*args)


def mean_kernel(
    info_ref, own_ref, came_ref, link_ref, last_ref,
    mean_ref, out_link_ref,
    mean_all, col_all, border, *, scale, count, masks,
):
    stride = 2 * count + 8
    half = (own_ref.shape[0] - SENT) // stride
    place, core = info_ref[0], info_ref[1]
    for d in range(2 * half):
        owner = place ^ jnp.where(core == 0, masks[0][d], masks[1][d])
        ref = own_ref if d < half else came_ref
        base = SENT + (d % half) * stride
        block = ref[base : base + stride, :].astype(f32)
        at = pl.ds(pl.multiple_of(owner * count, 8), count)
        mean_all[at, :] = block[0:count]
        col_all[at, :] = block[count : 2 * count]
        border[pl.ds(pl.multiple_of(owner * 8, 8), 8), :] = block[2 * count :]
    mean_ref[...] = scale * dot(mean_all[...].astype(bf16), col_all[...].astype(bf16), 0, 0)
    out_link_ref[...] = link_ref[...]
    pieces = border[pl.ds(pl.multiple_of(jnp.minimum(place + 1, 2 * half - 1) * 8, 8), 8), :]
    point = pieces[0:3, 0:128] + pieces[0:3, 128:] + pieces[3:6, 0:128]
    jump = point + last_ref[0:3, :]
    total = jnp.sum(jump * jump, axis=0, keepdims=True) * (1.0 / (12.0 * step_tau))
    out_link_ref[count - 1 : count, :] = jnp.where(place == 2 * half - 1, 0.0, total)


def mean_call(info, own, came, link, last, scale, count, masks):
    args = (info, near(own), near(came), near(link), near(last))
    devices = len(masks[0])

    def body(*refs):
        mean_kernel(*refs, scale=scale, count=count, masks=masks)

    return pl.pallas_call(
        body,
        in_specs=[SMEM] + [VMEM] * 4,
        out_specs=[VMEM] * 2,
        out_shape=[
            jax.ShapeDtypeStruct((256, 256), f32),
            jax.ShapeDtypeStruct((count, 128), f32),
        ],
        scratch_shapes=[
            pltpu.VMEM((devices * count, 256), f32),
            pltpu.VMEM((devices * count, 256), f32),
            pltpu.VMEM((devices * 8, 256), f32),
        ],
        compiler_params=PARAMS,
        name="mean_and_link",
    )(*args)


def end_kernel(core_ref, own_ref, came_ref, one_ref, pool_ref, pair_ref, bias_ref, *, scale):
    def write(low_ref, high_ref):
        one_ref[0:ONE, :] = scale * low_ref[0:ONE, :]
        one_ref[ONE:, :] = scale * high_ref[0:ONE, :]
        pool_ref[0:POOL, :] = scale * low_ref[ONE : ONE + POOL, :]
        pool_ref[POOL:, :] = scale * high_ref[ONE : ONE + POOL, :]

        small = low_ref[ONE + POOL : HALF, :]
        rows = jnp.concatenate(
            [jnp.broadcast_to(small[r : r + 1], (8, 256)) for r in range(4)], axis=0
        )
        rows = jnp.where(iota((32, 256), 0) % 8 == iota((32, 256), 1) // 32, rows, 0.0)
        total = rows[:, 0:128] + rows[:, 128:]
        total = total + pltpu.roll(total, 64, 1)
        total = total + pltpu.roll(total, 32, 1)
        pair_ref[...] = (scale / 256.0) * total[:, 0:32].T
        bias_ref[...] = (scale / 256.0) * small[4:5, 0:32]

    core = core_ref[0]
    pl.when(core == 0)(lambda: write(own_ref, came_ref))
    pl.when(core == 1)(lambda: write(came_ref, own_ref))


def end_call(core, own, came, scale):
    def body(*refs):
        end_kernel(*refs, scale=scale)

    return pl.pallas_call(
        body,
        in_specs=[SMEM, VMEM, VMEM],
        out_specs=[VMEM] * 4,
        out_shape=[
            jax.ShapeDtypeStruct((256, 256), f32),
            jax.ShapeDtypeStruct((32, 256), f32),
            jax.ShapeDtypeStruct((32, 32), f32),
            jax.ShapeDtypeStruct((1, 32), f32),
        ],
        compiler_params=PARAMS,
        name="unpack",
    )(core, near(own), near(came))


def local(
    positions, hidden, cotangent, embed_weight, embed_bias, pair_weight, pair_bias,
    one_weight, pool_weight, mean_weight, one_bias, drift_weight,
):
    count, own_count, width = hidden.shape
    slices = lax.axis_size("slices")
    bits = slices.bit_length() - 1
    scale = 1.0 / math.sqrt(count * slices * own_count * lax.axis_size("ering"))
    core = lax.axis_index("ering").astype(jnp.int32)
    place = lax.axis_index("slices").astype(jnp.int32)

    def swap(array):
        return lax.ppermute(array, "ering", [(0, 1), (1, 0)])

    orders = [[(t + e) % bits for t in range(bits)] for e in range(2)]
    masks = [
        [sum(((d >> t) & 1) << orders[e][t] for t in range(bits)) for d in range(slices)]
        for e in range(2)
    ]
    info = jnp.stack([place, core])
    core = core.reshape(1)

    other_pos = swap(positions)
    part_sum = jnp.sum(hidden.astype(f32), axis=1)
    other_sum = swap(part_sum)
    pooled, h_sums, g_sums, one_pre, hid_near, cot_near, one_near, pool_near, mean_near = pair_call(
        positions, other_pos, embed_weight, embed_bias, pair_weight, pair_bias,
        (hidden, cotangent, one_weight, pool_weight, mean_weight),
    )
    updated, pre, keep, send, mean_rows = one_call(
        core, hid_near, cot_near, one_pre, pooled, h_sums, g_sums, part_sum, other_sum,
        pool_near, mean_near, one_bias,
    )
    state, col_total = first_call(keep, swap(send), mean_rows, positions)
    hidden_grad, updated, link, last = back_call(
        cot_near.reshape(pre.shape), pre, updated, col_total, positions, one_near,
        mean_near, drift_weight,
    )
    for t in range(bits):
        pairs = [
            (s * 2 + e, (s ^ (1 << orders[e][t])) * 2 + e) for s in range(slices) for e in range(2)
        ]
        came = lax.ppermute(state, ("slices", "ering"), pairs)
        if t == bits - 1:
            came, hidden_grad, link, last = lax.optimization_barrier((came, hidden_grad, link, last))
        if t < bits - 1:
            state = mix_call(state, came)
    total = last_call(state, came)
    other_total = swap(total)
    mean_grad, link_terms = mean_call(info, state, came, link, last, scale, count, masks)
    one_grad, pool_grad, pair_grad, bias_grad = end_call(core, total, other_total, scale)
    return (
        updated.reshape(hidden.shape),
        hidden_grad.reshape(hidden.shape),
        link_terms,
        pair_grad,
        bias_grad.reshape(-1),
        one_grad,
        pool_grad,
        mean_grad,
    )


def solution(mesh):
    in_specs = (
        P(None, ("groups", "slices"), "ering"),
        P(("groups", "slices"), "ering", None),
        P(("groups", "slices"), "ering", None),
    ) + (P(),) * 9
    out_specs = (
        P(("groups", "slices"), "ering", None),
        P(("groups", "slices"), "ering", None),
        P(("groups", "slices"), "ering"),
        P("groups", None),
        P("groups"),
        P("groups", None),
        P("groups", None),
        P("groups", None),
    )
    return jax.shard_map(local, mesh=mesh, in_specs=in_specs, out_specs=out_specs, check_vma=False)
```

```python
import math

import jax
import jax.numpy as jnp
from jax import lax
from jax.experimental import pallas as pl
from jax.experimental.pallas import tpu as pltpu
from jax.sharding import PartitionSpec as P

HIGH = lax.Precision.HIGHEST
f32 = jnp.float32
bf16 = jnp.bfloat16
step_tau = 0.5
ONE, POOL, SMALL = 128, 16, 8
HALF = ONE + POOL + SMALL
SENT = HALF + SMALL
COPIED = 5
PARAMS = pltpu.CompilerParams(vmem_limit_bytes=16 << 20)
VMEM = pl.BlockSpec(memory_space=pltpu.VMEM)
SMEM = pl.BlockSpec(memory_space=pltpu.SMEM)


def near(array):
    return pltpu.with_memory_space_constraint(array, pltpu.VMEM)


def far(array):
    return pltpu.with_memory_space_constraint(array, pltpu.HBM)


def dot(a, b, ca, cb, precision=None):
    return lax.dot_general(
        a, b, (((ca,), (cb,)), ((), ())), preferred_element_type=f32, precision=precision
    )


def split3(x):
    first = x.astype(bf16).astype(f32)
    rest = x - first
    second = rest.astype(bf16).astype(f32)
    return first, second, rest - second


def iota(shape, dim):
    return lax.broadcasted_iota(jnp.int32, shape, dim)


def pair_kernel(
    own_ref, other_ref, ew_ref, eb_ref, pw_ref, pb_ref, *refs
):
    pooled_ref, h_ref, g_ref, pre_ref = refs[COPIED : COPIED + 4]
    near_refs = refs[COPIED + 4 : 2 * COPIED + 4]
    copies = [
        pltpu.make_async_copy(refs[n], near_refs[n], refs[-1].at[n]) for n in range(COPIED)
    ]
    for copy in copies:
        copy.start()

    def ready():
        for copy in copies:
            copy.wait()

    def weigh(step):
        at = pl.ds(2 * step, 2)
        rows = near_refs[0][at].reshape(256, 256)
        pre_ref[at] = dot(rows, near_refs[2][...], 1, 0).reshape(2, 128, 256)

    pair_steps(
        own_ref, other_ref, ew_ref, eb_ref, pw_ref, pb_ref, pooled_ref, h_ref, g_ref,
        ready, weigh, *refs[2 * COPIED + 4 : -1],
    )


def pair_steps(
    own_ref, other_ref, ew_ref, eb_ref, pw_ref, pb_ref,
    pooled_ref, h_ref, g_ref, ready, weigh,
    embed_mat, block_mat, a_rows, feat_a, feat_b, bias_row,
    pre_a, pre_b, act_a, act_b, in_a, in_b, in_c, in_d, slope_a, slope_b, sum_a, sum_b, sum_c, sum_d,
):
    count = own_ref.shape[1]
    feats = (feat_a, feat_b)
    pre, acts, slopes = (pre_a, pre_b), (act_a, act_b), (slope_a, slope_b)
    ins, sums = (in_a, in_b, in_c, in_d), (sum_a, sum_b, sum_c, sum_d)

    def features(feat, at):
        size = 256
        points = [
            jnp.concatenate([ref[c, pl.ds(at, 1), :] for ref in (own_ref, other_ref)], axis=1)
            for c in range(3)
        ]
        columns = jnp.concatenate(points + [jnp.zeros((5, 256), f32)], axis=0).T
        misc = jnp.zeros((24, 256), f32)
        row = iota((24, 256), 0)
        for c in range(3):
            s1, s2, s3 = split3(points[c])
            for p, piece in enumerate((s1, s1, s1, s2, s2, s3)):
                misc = jnp.where(row == 6 * c + p, piece, misc)
        zeros = jnp.zeros((64, 256), f32)
        misc = jnp.concatenate([zeros, misc, zeros[0:40]], axis=0).T
        lane = iota((size, 128), 1)
        square = jnp.ones((size, 128), f32)
        for c in range(3):
            spread = jnp.broadcast_to(columns[:, c : c + 1], (size, 128))
            offset = spread - own_ref[c, pl.ds(at, 1), :]
            square = square + offset * offset
        radial = square * lax.rsqrt(square)
        high = radial.astype(bf16).astype(f32)
        low = radial - high
        high_turned = pltpu.roll(high, 64, 1)
        low_turned = pltpu.roll(low, 64, 1)
        left = lane < 64
        feat[0, :, :128] = jnp.where(left, high, low_turned).astype(bf16)
        feat[0, :, 128:] = jnp.where(left, high, misc).astype(bf16)
        feat[1, :, :128] = jnp.where(left, high_turned, low).astype(bf16)
        feat[1, :, 128:] = jnp.where(left, high_turned, misc).astype(bf16)

    wide = jnp.concatenate([ew_ref[...]] * 8, axis=1)
    w1, w2, w3 = split3(wide)
    row = iota((64, 256), 0)
    lane = iota((64, 256), 1)
    pieces = (w1, w2, w3, w1, w2, w1)
    misc = jnp.zeros((64, 256), f32)
    for c in range(3):
        for p in range(6):
            misc = jnp.where(row == 6 * c + p, -pieces[p][c : c + 1, :], misc)
    misc = misc.astype(bf16)
    for g in range(8):
        hit = row == g * 8 + lane // 32
        first = jnp.where(hit, w1[3:4, :], 0.0).astype(bf16)
        embed_mat[0:64, g * 256 : (g + 1) * 256] = first
        embed_mat[64:128, g * 256 : (g + 1) * 256] = first
        embed_mat[128:192, g * 256 : (g + 1) * 256] = jnp.where(hit, w2[3:4, :], 0.0).astype(bf16)
        embed_mat[192:256, g * 256 : (g + 1) * 256] = misc
    row = iota((256, 256), 0)
    lane = iota((256, 256), 1)
    tiled = jnp.concatenate([pw_ref[...].astype(f32).T] * 8, axis=1)
    tiled = jnp.concatenate([tiled] * 8, axis=0)
    block_mat[...] = jnp.where(row // 32 == lane // 32, tiled, 0.0).astype(bf16)
    bias_row[...] = jnp.broadcast_to(jnp.concatenate([pb_ref[...]] * 8, axis=1), (8, 256))
    wide_bias = jnp.concatenate([eb_ref[...]] * 8, axis=1)
    electron = iota((128, 256), 0)
    lane128 = iota((128, 256), 1)
    points = jnp.concatenate(
        [piece for c in range(3) for piece in split3(own_ref[c])], axis=0
    ).astype(bf16)
    for g in range(16):
        pick = jnp.where(electron == g * 8 + lane128 // 32, 1.0, 0.0).astype(bf16)
        spread = dot(points, pick, 1, 0)
        total = jnp.broadcast_to(wide_bias, (count, 256))
        for c in range(3):
            base = 3 * c * count
            point = (
                spread[base : base + count]
                + spread[base + count : base + 2 * count]
                + spread[base + 2 * count : base + 3 * count]
            )
            total = total + point * wide[c : c + 1, :]
        a_rows[:, g * 256 : (g + 1) * 256] = total
    features(feat_a, 0)
    diagonal = iota((8, 256), 0) == iota((8, 256), 1) // 32
    block = iota((32, 256), 1) // 32

    def turn(step, places, started):
        def embed(n):
            at = 2 * step + n // 16
            half, inner = n % 16 // 8, n % 8
            out = dot(feats[n // 16][half], embed_mat[:, inner * 256 : (inner + 1) * 256], 1, 0)
            pre[n % 2][...] = out + a_rows[pl.ds(at, 1), n % 16 * 256 : (n % 16 + 1) * 256]

        def first_tanh(n):
            out = jnp.tanh(pre[n % 2][...])
            ins[n % 4][...] = out.astype(bf16)
            sums[n % 4][...] = jnp.sum(out.reshape(32, 8, 256), axis=0)

        def layer(n):
            acts[n % 2][...] = dot(ins[n % 4][...], block_mat[...], 1, 0) + bias_row[0:1, :]

        def slice_of(n):
            return jnp.maximum(2 * step - 1, 0) if n < 0 else 2 * step + n // 16

        def second_tanh(n):
            at, g = slice_of(n), n % 16
            act = jnp.tanh(acts[n % 2][...])
            total = sums[n % 4][...] + jnp.sum(act.reshape(32, 8, 256), axis=0)
            mean = jnp.sum(total, axis=0, keepdims=True) * (1.0 / 256)
            slope = 1.0 - act * act
            h_ref[at, g : g + 1, :] = jnp.sum(slope, axis=0, keepdims=True)
            pooled_ref[at, g * 8 : (g + 1) * 8, :] = jnp.where(diagonal, mean, 0.0)
            slopes[n % 2][...] = slope.astype(bf16)

        def outer(n):
            at, g = slice_of(n), n % 16
            product = dot(ins[n % 4][...], slopes[n % 2][...], 0, 0)
            picked = product[0:32]
            for q in range(1, 8):
                picked = jnp.where(block == q, product[q * 32 : (q + 1) * 32], picked)
            g_ref[at, g * 32 : (g + 1) * 32, :] = picked

        for place in places:
            for lag, stage in enumerate((embed, first_tanh, layer, second_tanh, outer)):
                if place - lag < started:
                    stage(place - lag)
            if started and place % 16 == 0:
                upcoming = jnp.minimum(2 * step + place // 16 + 1, count - 1)
                features(feats[1 - place // 16], upcoming)

    turns = count // 2

    def body(step, carry):
        pl.when(step == 1)(ready)
        pl.when(step >= 1)(lambda: weigh(step - 1))
        turn(step, range(32), 32)
        return carry

    lax.fori_loop(0, turns, body, 0)
    if turns == 1:
        ready()
    weigh(turns - 1)
    turn(turns, range(4), 0)


def pair_call(own, other, ew, eb, pw, pb, later):
    count = own.shape[1]
    args = (
        far(own), near(other), far(ew.T), far(eb.reshape(1, 32)), far(pw), far(pb.reshape(1, 32)),
    ) + tuple(far(a) for a in later)
    return pl.pallas_call(
        pair_kernel,
        in_specs=[VMEM] * 6 + [pl.BlockSpec(memory_space=pltpu.HBM)] * COPIED,
        out_specs=[VMEM] * (4 + COPIED),
        out_shape=[
            pltpu.VMEM((count, 128, 256), f32),
            pltpu.VMEM((count, 16, 256), f32),
            pltpu.VMEM((count, 512, 256), f32),
            pltpu.VMEM((count, 128, 256), f32),
        ]
        + [pltpu.VMEM(a.shape, a.dtype) for a in later],
        scratch_shapes=[
            pltpu.VMEM((256, 2048), bf16),
            pltpu.VMEM((256, 256), bf16),
            pltpu.VMEM((count, 4096), f32),
            pltpu.VMEM((2, 256, 256), bf16),
            pltpu.VMEM((2, 256, 256), bf16),
            pltpu.VMEM((8, 256), f32),
        ]
        + [pltpu.VMEM((256, 256), f32)] * 4
        + [pltpu.VMEM((256, 256), bf16)] * 6
        + [pltpu.VMEM((8, 256), f32)] * 4
        + [pltpu.SemaphoreType.DMA((COPIED,))],
        compiler_params=pltpu.CompilerParams(vmem_limit_bytes=24 << 20),
        name="pair_stage",
    )(*args)


def one_kernel(
    core_ref, hid_ref, cot_ref, one_pre_ref, pooled_ref, h_ref, g_ref, sum_a_ref, sum_b_ref,
    qw_ref, mw_ref, ob_ref,
    updated_ref, grad_ref, keep_ref, send_ref, mean_ref,
    back_all,
):
    count = sum_a_ref.shape[0]
    pool_mat = jnp.concatenate([qw_ref[...]] * 8, axis=0)
    mean_rows = ((sum_a_ref[...] + sum_b_ref[...]) * (1.0 / 256)).astype(bf16)
    mean_ref[...] = mean_rows
    per_slice = dot(mean_rows, mw_ref[...], 1, 0) + ob_ref[...]
    own_lanes = iota((256, 256), 0) % 8 == iota((256, 256), 1) // 32
    one_total = jnp.zeros((256, 256), f32)
    pool_total = jnp.zeros((256, 256), f32)
    pair_total = jnp.zeros((32, 256), f32)
    bias_total = jnp.zeros((32, 256), f32)
    parts = []

    def two(ref, n):
        value = ref[2 * n : 2 * n + 2]
        return value.reshape(2 * value.shape[1], 256)

    for step in range(count // 2 + 2):
        if step < count // 2:
            rows = slice(step * 256, (step + 1) * 256)
            shift = jnp.concatenate(
                [
                    jnp.broadcast_to(per_slice[n : n + 1, :], (128, 256))
                    for n in (2 * step, 2 * step + 1)
                ],
                axis=0,
            )
            pooled = two(pooled_ref, step).astype(bf16)
            act = jnp.tanh(two(one_pre_ref, step) + dot(pooled, pool_mat, 1, 0) + shift)
            updated_ref[rows, :] = (act + two(hid_ref, step).astype(f32)).astype(bf16)
            grad = (two(cot_ref, step).astype(f32) * (1.0 - act * act)).astype(bf16)
            grad_ref[rows, :] = grad
            wide = grad.astype(f32)
            parts.append(jnp.sum(wide[0:128], axis=0, keepdims=True))
            parts.append(jnp.sum(wide[128:], axis=0, keepdims=True))
        n = step - 1
        if 0 <= n < count // 2:
            grad = grad_ref[n * 256 : (n + 1) * 256, :]
            back = jnp.where(own_lanes, dot(grad, pool_mat, 1, 1), 0.0)
            back_all[n] = jnp.sum(back.reshape(32, 8, 256), axis=1)
            one_total = one_total + dot(two(hid_ref, n), grad, 0, 0)
            pool_total = pool_total + dot(two(pooled_ref, n).astype(bf16), grad, 0, 0)
        n = step - 2
        if 0 <= n < count // 2:
            bias_total = bias_total + back_all[n] * two(h_ref, n)
            for g in range(32):
                part = g_ref[2 * n + g // 16, g % 16 * 32 : (g % 16 + 1) * 32, :]
                pair_total = pair_total + part * back_all[n, g : g + 1, :]
    pool = pool_total[0:32]
    for q in range(1, 8):
        pool = pool + pool_total[q * 32 : (q + 1) * 32]
    bias_one = jnp.broadcast_to(jnp.sum(bias_total, axis=0, keepdims=True), (8, 256))
    folded = jnp.concatenate([pair_total, bias_one], axis=0)
    folded = folded[:, 0:128] + folded[:, 128:]
    folded = folded + pltpu.roll(folded, 64, 1)
    folded = folded + pltpu.roll(folded, 32, 1)
    folded = jnp.concatenate([folded, folded], axis=1)
    picked = jnp.where(iota((32, 256), 0) % 8 == iota((32, 256), 1) // 32, folded[0:32], 0.0)
    packed = jnp.sum(picked.reshape(4, 8, 256), axis=1)
    small = jnp.concatenate([packed, folded[32:36]], axis=0)
    core = core_ref[0]

    @pl.when(core == 0)
    def _():
        keep_ref[0:ONE, :] = one_total[0:ONE]
        send_ref[0:ONE, :] = one_total[ONE:]
        keep_ref[ONE : ONE + POOL, :] = pool[0:POOL]
        send_ref[ONE : ONE + POOL, :] = pool[POOL:]

    @pl.when(core == 1)
    def _():
        send_ref[0:ONE, :] = one_total[0:ONE]
        keep_ref[0:ONE, :] = one_total[ONE:]
        send_ref[ONE : ONE + POOL, :] = pool[0:POOL]
        keep_ref[ONE : ONE + POOL, :] = pool[POOL:]

    keep_ref[ONE + POOL : HALF, :] = small
    send_ref[ONE + POOL : HALF, :] = small
    sums = jnp.concatenate(parts, axis=0)
    keep_ref[HALF:, :] = sums
    send_ref[HALF:, :] = sums


def one_call(core, hid, cot, one_pre, pooled, h_sums, g_sums, sum_a, sum_b, qw, mw, ob):
    count, rows, width = hid.shape
    args = (
        core, near(hid), near(cot), near(one_pre), near(pooled), near(h_sums), near(g_sums), near(sum_a),
        near(sum_b), near(qw), near(mw), far(ob.reshape(1, width)),
    )
    return pl.pallas_call(
        one_kernel,
        in_specs=[SMEM] + [VMEM] * 11,
        out_specs=[VMEM] * 5,
        out_shape=[
            pltpu.VMEM((count * rows, width), bf16),
            pltpu.VMEM((count * rows, width), bf16),
            pltpu.VMEM((HALF + count, width), f32),
            pltpu.VMEM((HALF + count, width), f32),
            pltpu.VMEM((count, width), bf16),
        ],
        scratch_shapes=[pltpu.VMEM((count // 2, 32, 256), f32)],
        compiler_params=PARAMS,
        name="one_stage",
    )(*args)


def pack(total, gath, out_ref):
    out_ref[0:HALF, :] = total.astype(bf16)
    small = total[ONE + POOL :]
    out_ref[HALF:SENT, :] = (small - small.astype(bf16).astype(f32)).astype(bf16)
    at = SENT
    for piece in gath:
        out_ref[at : at + piece.shape[0], :] = piece
        at += piece.shape[0]


def first_kernel(keep_ref, came_ref, mean_ref, pos_ref, out_ref, col_ref):
    both = keep_ref[...] + came_ref[...]
    col = both[HALF:]
    col_ref[...] = col
    p1, p2, p3 = split3(pos_ref[:, 0, :])
    blank = jnp.zeros((2, 256), f32)
    border = jnp.concatenate(
        [
            jnp.concatenate([p1, p2], axis=1),
            jnp.concatenate([p3, jnp.zeros_like(p3)], axis=1),
            blank,
        ],
        axis=0,
    )
    gath = jnp.concatenate([mean_ref[...].astype(f32), col, border], axis=0).astype(bf16)
    pack(both[0:HALF], [gath], out_ref)


def first_call(keep, came, mean_rows, pos):
    count = mean_rows.shape[0]
    return pl.pallas_call(
        first_kernel,
        in_specs=[VMEM] * 4,
        out_specs=[VMEM] * 2,
        out_shape=[
            pltpu.VMEM((SENT + 2 * count + 8, 256), bf16),
            pltpu.VMEM((count, 256), f32),
        ],
        compiler_params=PARAMS,
        name="first_mix",
    )(near(keep), near(came), near(mean_rows), pos)


def add_up(own_ref, came_ref):
    total = own_ref[0:HALF, :].astype(f32) + came_ref[0:HALF, :].astype(f32)
    rest = own_ref[HALF:SENT, :].astype(f32) + came_ref[HALF:SENT, :].astype(f32)
    return jnp.concatenate([total[0 : ONE + POOL], total[ONE + POOL :] + rest], axis=0)


def mix_kernel(own_ref, came_ref, out_ref):
    pack(add_up(own_ref, came_ref), [own_ref[SENT:, :], came_ref[SENT:, :]], out_ref)


def mix_call(own, came):
    rows = SENT + 2 * (own.shape[0] - SENT)
    return pl.pallas_call(
        mix_kernel,
        in_specs=[VMEM] * 2,
        out_specs=VMEM,
        out_shape=pltpu.VMEM((rows, 256), bf16),
        compiler_params=PARAMS,
        name="mix",
    )(near(own), near(came))


def last_kernel(own_ref, came_ref, out_ref):
    out_ref[...] = add_up(own_ref, came_ref)


def last_call(own, came):
    return pl.pallas_call(
        last_kernel,
        in_specs=[VMEM] * 2,
        out_specs=VMEM,
        out_shape=pltpu.VMEM((HALF, 256), f32),
        compiler_params=PARAMS,
        name="last_mix",
    )(near(own), near(came))


def back_kernel(
    cot_ref, pre_ref, upd_ref, col_ref, pos_ref, ow_ref, mw_ref, dw_ref,
    grad_ref, out_ref, link_ref, last_ref,
):
    count = col_ref.shape[0]
    back = dot(col_ref[...], mw_ref[...].astype(f32), 1, 1, HIGH) * (1.0 / 256)
    drifts = []
    for s in range(count):
        at = slice(s * 128, (s + 1) * 128)
        grad = cot_ref[at, :].astype(f32) + dot(pre_ref[at, :], ow_ref[...], 1, 1)
        grad_ref[at, :] = (grad + back[s : s + 1, :]).astype(bf16)
        drifts.append(dot(dw_ref[...], upd_ref[at, :], 1, 1))
        out_ref[at, :] = upd_ref[at, :]
    for s in range(count):
        here = [-pos_ref[c, s : s + 1, :] - step_tau * drifts[s][c : c + 1, :] for c in range(3)]
        if s < count - 1:
            jumps = [here[c] + pos_ref[c, s + 1 : s + 2, :] for c in range(3)]
            total = jumps[0] * jumps[0] + jumps[1] * jumps[1] + jumps[2] * jumps[2]
            link_ref[s : s + 1, :] = total * (1.0 / (12.0 * step_tau))
        else:
            link_ref[s : s + 1, :] = jnp.zeros((1, 128), f32)
            last_ref[...] = jnp.concatenate(here + [jnp.zeros((5, 128), f32)], axis=0)


def back_call(cot, pre, updated, col, pos, ow, mw, dw):
    args = (near(cot), near(pre), near(updated), near(col), far(pos), near(ow), near(mw), far(dw))
    return pl.pallas_call(
        back_kernel,
        in_specs=[VMEM] * len(args),
        out_specs=[VMEM] * 4,
        out_shape=[
            jax.ShapeDtypeStruct(cot.shape, bf16),
            jax.ShapeDtypeStruct(cot.shape, bf16),
            pltpu.VMEM((col.shape[0], 128), f32),
            pltpu.VMEM((8, 128), f32),
        ],
        compiler_params=PARAMS,
        name="hidden_back",
    )(*args)


def mean_kernel(
    place_ref, core_ref, own_ref, came_ref, link_ref, last_ref,
    mean_ref, out_link_ref,
    mean_all, col_all, border, *, scale, count, masks,
):
    stride = 2 * count + 8
    half = (own_ref.shape[0] - SENT) // stride
    place, core = place_ref[0], core_ref[0]
    for d in range(2 * half):
        owner = place ^ jnp.where(core == 0, masks[0][d], masks[1][d])
        ref = own_ref if d < half else came_ref
        base = SENT + (d % half) * stride
        block = ref[base : base + stride, :].astype(f32)
        at = pl.ds(pl.multiple_of(owner * count, 8), count)
        mean_all[at, :] = block[0:count]
        col_all[at, :] = block[count : 2 * count]
        border[pl.ds(pl.multiple_of(owner * 8, 8), 8), :] = block[2 * count :]
    mean_ref[...] = scale * dot(mean_all[...].astype(bf16), col_all[...].astype(bf16), 0, 0)
    out_link_ref[...] = link_ref[...]
    pieces = border[pl.ds(pl.multiple_of(jnp.minimum(place + 1, 2 * half - 1) * 8, 8), 8), :]
    point = pieces[0:3, 0:128] + pieces[0:3, 128:] + pieces[3:6, 0:128]
    jump = point + last_ref[0:3, :]
    total = jnp.sum(jump * jump, axis=0, keepdims=True) * (1.0 / (12.0 * step_tau))
    out_link_ref[count - 1 : count, :] = jnp.where(place == 2 * half - 1, 0.0, total)


def mean_call(place, core, own, came, link, last, scale, count, masks):
    args = (place, core, near(own), near(came), near(link), near(last))
    devices = len(masks[0])

    def body(*refs):
        mean_kernel(*refs, scale=scale, count=count, masks=masks)

    return pl.pallas_call(
        body,
        in_specs=[SMEM] * 2 + [VMEM] * 4,
        out_specs=[VMEM] * 2,
        out_shape=[
            jax.ShapeDtypeStruct((256, 256), f32),
            jax.ShapeDtypeStruct((count, 128), f32),
        ],
        scratch_shapes=[
            pltpu.VMEM((devices * count, 256), f32),
            pltpu.VMEM((devices * count, 256), f32),
            pltpu.VMEM((devices * 8, 256), f32),
        ],
        compiler_params=PARAMS,
        name="mean_and_link",
    )(*args)


def end_kernel(core_ref, own_ref, came_ref, one_ref, pool_ref, pair_ref, bias_ref, *, scale):
    def write(low_ref, high_ref):
        one_ref[0:ONE, :] = scale * low_ref[0:ONE, :]
        one_ref[ONE:, :] = scale * high_ref[0:ONE, :]
        pool_ref[0:POOL, :] = scale * low_ref[ONE : ONE + POOL, :]
        pool_ref[POOL:, :] = scale * high_ref[ONE : ONE + POOL, :]

        small = low_ref[ONE + POOL : HALF, :]
        rows = jnp.concatenate(
            [jnp.broadcast_to(small[r : r + 1], (8, 256)) for r in range(4)], axis=0
        )
        rows = jnp.where(iota((32, 256), 0) % 8 == iota((32, 256), 1) // 32, rows, 0.0)
        total = rows[:, 0:128] + rows[:, 128:]
        total = total + pltpu.roll(total, 64, 1)
        total = total + pltpu.roll(total, 32, 1)
        pair_ref[...] = (scale / 256.0) * total[:, 0:32].T
        bias_ref[...] = (scale / 256.0) * small[4:5, 0:32]

    core = core_ref[0]
    pl.when(core == 0)(lambda: write(own_ref, came_ref))
    pl.when(core == 1)(lambda: write(came_ref, own_ref))


def end_call(core, own, came, scale):
    def body(*refs):
        end_kernel(*refs, scale=scale)

    return pl.pallas_call(
        body,
        in_specs=[SMEM, VMEM, VMEM],
        out_specs=[VMEM] * 4,
        out_shape=[
            jax.ShapeDtypeStruct((256, 256), f32),
            jax.ShapeDtypeStruct((32, 256), f32),
            jax.ShapeDtypeStruct((32, 32), f32),
            jax.ShapeDtypeStruct((1, 32), f32),
        ],
        compiler_params=PARAMS,
        name="unpack",
    )(core, near(own), near(came))


def local(
    positions, hidden, cotangent, embed_weight, embed_bias, pair_weight, pair_bias,
    one_weight, pool_weight, mean_weight, one_bias, drift_weight,
):
    count, own_count, width = hidden.shape
    slices = lax.axis_size("slices")
    bits = slices.bit_length() - 1
    scale = 1.0 / math.sqrt(count * slices * own_count * lax.axis_size("ering"))
    core = lax.axis_index("ering").astype(jnp.int32)
    place = lax.axis_index("slices").astype(jnp.int32)

    def swap(array):
        return lax.ppermute(array, "ering", [(0, 1), (1, 0)])

    orders = [[(t + e) % bits for t in range(bits)] for e in range(2)]
    masks = [
        [sum(((d >> t) & 1) << orders[e][t] for t in range(bits)) for d in range(slices)]
        for e in range(2)
    ]
    place = place.reshape(1)
    core = core.reshape(1)

    other_pos = swap(positions)
    part_sum = jnp.sum(hidden.astype(f32), axis=1)
    other_sum = swap(part_sum)
    pooled, h_sums, g_sums, one_pre, hid_near, cot_near, one_near, pool_near, mean_near = pair_call(
        positions, other_pos, embed_weight, embed_bias, pair_weight, pair_bias,
        (hidden, cotangent, one_weight, pool_weight, mean_weight),
    )
    updated, pre, keep, send, mean_rows = one_call(
        core, hid_near, cot_near, one_pre, pooled, h_sums, g_sums, part_sum, other_sum,
        pool_near, mean_near, one_bias,
    )
    state, col_total = first_call(keep, swap(send), mean_rows, positions)
    hidden_grad, updated, link, last = back_call(
        cot_near.reshape(pre.shape), pre, updated, col_total, positions, one_near,
        mean_near, drift_weight,
    )
    for t in range(bits):
        pairs = [
            (s * 2 + e, (s ^ (1 << orders[e][t])) * 2 + e) for s in range(slices) for e in range(2)
        ]
        came = lax.ppermute(state, ("slices", "ering"), pairs)
        if t == bits - 1:
            came, hidden_grad, link, last = lax.optimization_barrier((came, hidden_grad, link, last))
        if t < bits - 1:
            state = mix_call(state, came)
    total = last_call(state, came)
    other_total = swap(total)
    mean_grad, link_terms = mean_call(place, core, state, came, link, last, scale, count, masks)
    one_grad, pool_grad, pair_grad, bias_grad = end_call(core, total, other_total, scale)
    return (
        updated.reshape(hidden.shape),
        hidden_grad.reshape(hidden.shape),
        link_terms,
        pair_grad,
        bias_grad.reshape(-1),
        one_grad,
        pool_grad,
        mean_grad,
    )


def solution(mesh):
    in_specs = (
        P(None, ("groups", "slices"), "ering"),
        P(("groups", "slices"), "ering", None),
        P(("groups", "slices"), "ering", None),
    ) + (P(),) * 9
    out_specs = (
        P(("groups", "slices"), "ering", None),
        P(("groups", "slices"), "ering", None),
        P(("groups", "slices"), "ering"),
        P("groups", None),
        P("groups"),
        P("groups", None),
        P("groups", None),
        P("groups", None),
    )
    return jax.shard_map(local, mesh=mesh, in_specs=in_specs, out_specs=out_specs, check_vma=False)
```
